768 devices in a mesh: dp: 64 (over x, y, core), tensor: 12 (over z).
Axes of the slice: x: 4, y: 8, z: 12, core: 2. Of those that a mesh axis runs over, the one named last changes fastest.
Arguments:
- image_rows: bfloat16 [32768, 3072], P('dp'), may hold values from -6 to 6
- image_mod: float32 [64, 2, 3072], P('dp'), may hold values from -3 to 3
- caption_rows: bfloat16 [16384, 3072], P('dp'), may hold values from -6 to 6
- caption_mod: float32 [64, 2, 3072], replicated, may hold values from -3 to 3
- row_owner: int32 [16384, 1], P('dp'), may hold values from 0 to 63; in each aligned block of 256 rows (0 to 255, 256 to 511, ...) at most 8 rows name the same one
- w_img_qkv: bfloat16 [3072, 3, 3072], P('dp', None, 'tensor'), may hold values from -0.109375 to 0.109375
- w_txt_qkv: bfloat16 [3072, 3, 3072], P('dp', None, 'tensor'), may hold values from -0.109375 to 0.109375
- img_qk_gain: float32 [2, 128], replicated, may hold values from 0.5 to 3
- txt_qk_gain: float32 [2, 128], replicated, may hold values from 0.5 to 3
Outputs:
- image_attn: bfloat16 [32768, 3072], P('dp', 'tensor')
- caption_attn: bfloat16 [16384, 3072], P('dp', 'tensor')
The draws below stay inside these ranges and needn't reach their ends.
Inputs may be any that keep to these rules, and one draw needn't show every extreme that they name: `row_owner`: among the 256 caption tokens of one bin (aligned blocks of rows), no sample is named more than 8 times, a bound that some block reaches.
All inputs are finite; a program needn't handle non-finite values.
Results may differ from the reference program's by a relative error of at most 0.012.
The reference program's roundings to bfloat16 on the way count: a program that leaves them out, or rounds other values in their place, can miss the bound.
Values may be sent and summed in bfloat16 or wider, within the bound.
A program may use at most 64 MiB of HBM per device.

```python
import math
import jax
import jax.numpy as jnp
import numpy as np
from jax import lax

D = 3072
HEADS = 24
HD = 128
IMG = 512
BIN = 256
SAMPLES = 64
SLOT = 8
CAPMAX = 512
N_DP = 64


def level_of(rng, shape, pieces, smallest, top_value):
    level, own = 1.0, jax.random.fold_in(rng, 6)
    for axis_at, shards_of in pieces:
        draws = jnp.exp(jax.random.uniform(jax.random.fold_in(own, axis_at), (shards_of,), jnp.float32, smallest / len(pieces), top_value / len(pieces)))
        level = level * jnp.repeat(draws, shape[axis_at] // shards_of).reshape([-1 if axis == axis_at else 1 for axis in range(len(shape))])
    return level


def shared_out(stream_key, own, number, rows, count, top, reach, lean):
    ranking = jax.random.permutation(stream_key, count)
    crowded, ordinary = load_shares(count, rows * top, reach, lean, True), load_shares(count, rows * top, reach, lean, False)
    places = jnp.arange(count)

    def named(tallies, rotation):
        used = int((tallies > 0).sum())
        fixed = max(1, used // 4)
        moved = fixed + (places - fixed + rotation * (used - fixed)) % max(1, count - fixed)
        return jnp.zeros((count,), jnp.int32).at[ranking[jnp.where(places < fixed, places, moved)]].set(jnp.asarray(tallies, jnp.int32))

    tallies = jnp.where(number % 4 == 0, named(crowded, number // 4), named(ordinary, number - number // 4 - 1))
    mixed = jax.random.permutation(jax.random.fold_in(own, 3), count)
    donor, taker = mixed[0:count // 2 * 2:2], mixed[1:count // 2 * 2:2]
    room = jnp.minimum(tallies[donor] - 1, reach - tallies[taker]) // 2
    room = jnp.where((donor == ranking[0]) | (taker == ranking[0]) | (tallies[taker] == 0), 0, jnp.maximum(room, 0))
    moved = jax.random.randint(jax.random.fold_in(own, 4), (count // 2,), 0, 1 << 20) % (room + 1)
    tallies = tallies.at[donor].add(-moved).at[taker].add(moved)
    items = jnp.searchsorted(jnp.cumsum(tallies), jnp.arange(rows * top), side="right").astype(jnp.int32)
    listing = items.reshape(top, rows).T
    listing = listing[jax.random.permutation(jax.random.fold_in(own, 1), rows)]
    rotation = jax.random.randint(jax.random.fold_in(own, 2), (rows, 1), 0, top)
    return jnp.take_along_axis(listing, (jnp.arange(top)[None, :] + rotation) % top, axis=1)


def load_shares(count, total, most, skew, full):
    loads = [(1 << 20) // math.isqrt(rank ** skew) + 1 for rank in range(1, count + 1)]
    largest = most if full else min(most, max(-(-total // count), total * loads[0] // sum(loads)))
    least = 1 if total - largest >= count - 1 else 0
    given, spare = [largest] + [least] * (count - 1), total - largest - least * (count - 1)
    while spare > 0:
        candidates = [i for i in range(1, count) if given[i] < largest] or [i for i in range(1, count) if given[i] < most]
        whole, budget = sum([loads[i] for i in candidates]), spare
        for i in candidates:
            addition = min(most - given[i], max(1, budget * loads[i] // whole), spare)
            given[i] = given[i] + addition
            spare = spare - addition
    return np.array(given)


def bell_draw(rng, dims, spread, limit, pieces=(), kind=jnp.bfloat16):
    factor_of = level_of(rng, dims, pieces, -0.22, 0.18) if pieces else 1.0
    values = jax.random.normal(rng, dims, jnp.float32) * spread * factor_of
    return jnp.minimum(jnp.maximum(values, -limit), limit).astype(kind)


def setup_inputs(seed: int = 0) -> dict:
    key_list = jax.random.split(jax.random.key(seed), 10)
    image_rows = bell_draw(key_list[0], (SAMPLES * IMG, D), 1.0, 6.0, ((0, 64),))
    image_mod = bell_draw(key_list[1], (SAMPLES, 2, D), 0.5, 3.0, ((0, 64),), jnp.float32)
    caption_rows = bell_draw(key_list[2], (SAMPLES * BIN, D), 1.0, 6.0, ((0, 64),))
    caption_mod = bell_draw(key_list[3], (SAMPLES, 2, D), 0.5, 3.0, (), jnp.float32)
    row_owner_keys = jax.random.split(jax.random.fold_in(key_list[4], 1), (SAMPLES * BIN) // BIN)
    row_owner_turns = jax.random.permutation(jax.random.fold_in(key_list[4], 3), (SAMPLES * BIN) // BIN)
    row_owner = jax.vmap(lambda own, number: shared_out(jax.random.fold_in(key_list[4], 2), own, number, BIN, N_DP, 1, SLOT, 2))(row_owner_keys, row_owner_turns).reshape((SAMPLES * BIN, 1))
    w_img_qkv = bell_draw(key_list[5], (D, 3, D), D ** -0.5, 0.109375, ((0, 64), (2, 12)))
    w_txt_qkv = bell_draw(key_list[6], (D, 3, D), D ** -0.5, 0.109375, ((0, 64), (2, 12)))
    img_qk_gain = jnp.clip(jnp.exp(jax.random.uniform(key_list[7], (2, HD), jnp.float32, math.log(0.5), math.log(3.0))), 0.5, 3.0)
    txt_qk_gain = jnp.clip(jnp.exp(jax.random.uniform(key_list[8], (2, HD), jnp.float32, math.log(0.5), math.log(3.0))), 0.5, 3.0)
    return dict(image_rows=image_rows, image_mod=image_mod, caption_rows=caption_rows, caption_mod=caption_mod, row_owner=row_owner, w_img_qkv=w_img_qkv, w_txt_qkv=w_txt_qkv, img_qk_gain=img_qk_gain, txt_qk_gain=txt_qk_gain)


def layer_norm(rows):
    values = rows.astype(jnp.float32)
    mean = lax.optimization_barrier(jnp.mean(values, axis=-1, keepdims=True))
    var = lax.optimization_barrier(jnp.mean((values - mean) ** 2, axis=-1, keepdims=True))
    return (values - mean) * lax.rsqrt(var + 1e-06)

def head_norm(values, gain):
    return values * lax.rsqrt(lax.optimization_barrier(jnp.mean(values * values, axis=-1, keepdims=True)) + 1e-06) * gain

def project(inputs, weight, gain):
    qkv = jnp.dot(inputs, weight.reshape(D, 3 * D), preferred_element_type=jnp.float32)
    qkv = qkv.reshape(inputs.shape[0], 3, HEADS, HD)
    query = head_norm(qkv[:, 0], gain[0]).astype(jnp.bfloat16)
    keys = head_norm(qkv[:, 1], gain[1]).astype(jnp.bfloat16)
    return (query, keys, qkv[:, 2].astype(jnp.bfloat16))

def reference(image_rows, image_mod, caption_rows, caption_mod, row_owner, w_img_qkv, w_txt_qkv, img_qk_gain, txt_qk_gain):
    img_norm = layer_norm(image_rows).reshape(SAMPLES, IMG, D)
    img_in = img_norm * (1.0 + image_mod[:, 1][:, None, :]) + image_mod[:, 0][:, None, :]
    img_in = img_in.reshape(SAMPLES * IMG, D).astype(jnp.bfloat16)
    owner = row_owner[:, 0].astype(jnp.int32)
    mods = caption_mod[owner]
    txt_in = (layer_norm(caption_rows) * (1.0 + mods[:, 1]) + mods[:, 0]).astype(jnp.bfloat16)
    iq, ik, iv = project(img_in, w_img_qkv, img_qk_gain)
    tq, tk, tv = project(txt_in, w_txt_qkv, txt_qk_gain)
    order = jnp.argsort(owner, stable=True).astype(jnp.int32)
    counts = lax.optimization_barrier(jnp.sum((owner[:, None] == jnp.arange(SAMPLES, dtype=jnp.int32)[None, :]).astype(jnp.int32), axis=0))
    starts = (jnp.cumsum(counts) - counts).astype(jnp.int32)
    padding = jnp.zeros((CAPMAX, HEADS, HD), jnp.bfloat16)
    sq = jnp.concatenate([tq[order], padding], axis=0)
    sk = jnp.concatenate([tk[order], padding], axis=0)
    sv = jnp.concatenate([tv[order], padding], axis=0)

    def one_sample(sample):
        begin = starts[sample]
        valid = jnp.arange(CAPMAX, dtype=jnp.int32) < counts[sample]
        first = (sample * IMG).astype(jnp.int32)
        query = jnp.concatenate([lax.dynamic_slice_in_dim(sq, begin, CAPMAX, 0), lax.dynamic_slice_in_dim(iq, first, IMG, 0)], axis=0)
        keys = jnp.concatenate([lax.dynamic_slice_in_dim(sk, begin, CAPMAX, 0), lax.dynamic_slice_in_dim(ik, first, IMG, 0)], axis=0)
        values = jnp.concatenate([lax.dynamic_slice_in_dim(sv, begin, CAPMAX, 0), lax.dynamic_slice_in_dim(iv, first, IMG, 0)], axis=0)
        live = jnp.concatenate([valid, jnp.ones((IMG,), bool)])
        scores = jnp.einsum('qhd,khd->hqk', query.astype(jnp.float32), keys.astype(jnp.float32)) / math.sqrt(HD)
        scores = jnp.where(live[None, None, :], scores, -jnp.inf)
        weights = jax.nn.softmax(scores, axis=-1).astype(jnp.bfloat16)
        result = jnp.einsum('hqk,khd->qhd', weights.astype(jnp.float32), values.astype(jnp.float32)).astype(jnp.bfloat16)
        return (result[:CAPMAX], result[CAPMAX:])
    cap_out, img_out = lax.map(one_sample, jnp.arange(SAMPLES, dtype=jnp.int32))
    image_attn = img_out.reshape(SAMPLES * IMG, D)
    place = jnp.zeros((SAMPLES * BIN,), jnp.int32).at[order].set(jnp.arange(SAMPLES * BIN, dtype=jnp.int32))
    rank = place - starts[owner]
    caption_attn = cap_out.reshape(SAMPLES * CAPMAX, D)[owner * CAPMAX + rank]
    return (image_attn, caption_attn)
```

```python
import functools
import math

import jax
import jax.numpy as jnp
from jax import lax
from jax.experimental import pallas as pl
from jax.experimental.pallas import tpu as pltpu
from jax.sharding import PartitionSpec as P

MESH = pl.DeviceIdType.MESH
HD = 128
NX, NY, NC = 4, 8, 2
N_DP = NX * NY * NC
F32 = jnp.float32
BF16 = jnp.bfloat16


def kernel(
    img_hbm, imod_ref, cap_hbm, cmod_hbm, owner_ref, wimg_hbm, wtxt_hbm, igain_ref, tgain_ref,
    oimg_ref, ocap_ref,
    img_v, cap_v, cmod_v, mod3, modrow, img_in, txt_in, wt, wi, picks, counts_out, counts_in,
    proj, payload, out_buf, in_buf, qkv, ret_out, ret_in, bias,
    loc_sem, rsem, ssem, asem,
):
    dp = lax.axis_index("dp")
    x, y, c = dp // (NY * NC), (dp // NC) % NY, dp % NC

    def at(xx, yy, cc):
        return (xx * NY + yy) * NC + cc

    def xs(d):
        return (x + d + NX) % NX

    def ys(d):
        return (y + d + NY) % NY

    dev = {
        "x+": at(xs(1), y, c), "x-": at(xs(-1), y, c),
        "y+": at(x, ys(1), c), "y-": at(x, ys(-1), c),
        "p": at(x, y, 1 - c),
    }
    weights = (wt, wi)

    loads = []
    for i, (src, dst) in enumerate((
        (wtxt_hbm, wt.at[x, y, c]), (wimg_hbm, wi.at[x, y, c]),
        (cmod_hbm, cmod_v), (cap_hbm, cap_v), (img_hbm, img_v),
    )):
        copy = pltpu.make_async_copy(src, dst, loc_sem.at[i])
        copy.start()
        loads.append(copy)

    barrier = pltpu.get_barrier_semaphore()
    for d in dev.values():
        pl.semaphore_signal(barrier, inc=1, device_id={"dp": d}, device_id_type=MESH)

    def ypiece(t, xx, yy):
        return weights[t].at[xx, yy, c, :, 16:48, :]

    def yhalf(t, xx, yy, h):
        return weights[t].at[xx, yy, c, :, 16 + 16 * h : 32 + 16 * h, :]

    def xpiece(t, xx, yy):
        return weights[t].at[xx, yy, c, :, 0:16, :]

    def xrow(t, yy, h):
        return weights[t].at[2 * h : 2 * h + 2, yy, c, :, 0:16, :]

    def ycol(t, xx):
        return weights[t].at[xx, :, c, :, 16:48, :]

    def ycolhalf(t, xx, h):
        return weights[t].at[xx, 4 * h : 4 * h + 4, c, :, 16:48, :]

    sent = []
    n_sent = [0, 0]
    names = {}

    def sem(t, name):
        key = names.setdefault(name, len(names))
        return rsem.at[t, key]

    def send(t, to, piece, name):
        copy = pltpu.make_async_remote_copy(
            src_ref=piece, dst_ref=piece, send_sem=ssem.at[t, n_sent[t]], recv_sem=sem(t, name),
            device_id={"dp": dev[to]}, device_id_type=MESH,
        )
        n_sent[t] += 1
        copy.start()
        sent.append(copy)

    def recv(t, piece, name):
        pltpu.make_async_copy(piece, piece, sem(t, name)).wait()

    def s0(t):
        own_y, own_x = ypiece(t, x, y), xpiece(t, x, y)
        send(t, "x+", own_x, "rx+")
        send(t, "x-", own_x, "rx-")
        send(t, "y+", own_y, "ry+1")
        send(t, "y-", own_y, "ry-1")
        send(t, "x+", own_y, "gx+")
        send(t, "x-", own_y, "gx-")
        send(t, "p", weights[t].at[x, y, c], "p")

    def r1(t):
        for s, d in (("+", -1), ("-", 1)):
            piece = xpiece(t, xs(d), y)
            recv(t, piece, "rx" + s)
            if s == "+-"[t]:
                send(t, "x" + s, piece, "rx2")
            send(t, "p", piece, "p")

    def r2(t):
        piece = xpiece(t, xs(2), y)
        recv(t, piece, "rx2")
        send(t, "p", piece, "p")

    def q0(t):
        for h in (0, 1):
            for s in "+-":
                send(t, "y" + s, xrow(t, y, h), f"qy{s}1{h}")

    def yphase(t, d):
        for s, m in (("+", -1), ("-", 1)):
            piece = ypiece(t, x, ys(m * d))
            recv(t, piece, f"ry{s}{d}")
            if d < 3:
                send(t, "y" + s, piece, f"ry{s}{d + 1}")
            else:
                h = "+-".index(s)
                send(t, "y" + s, yhalf(t, x, ys(m * d), h), f"ry{s}4")
            send(t, "p", piece, "p")

    def y4(t):
        for h, s in enumerate("+-"):
            recv(t, yhalf(t, x, ys(4), h), f"ry{s}4")
        send(t, "p", ypiece(t, x, ys(4)), "p")

    def xsend(t, *ds):
        for d in ds:
            for s in "+-":
                send(t, "x" + s, ypiece(t, x, ys(d)), "gx" + s)

    def qphase(t, d):
        for h in (0, 1):
            for s, m in (("+", -1), ("-", 1)):
                piece = xrow(t, ys(m * d), h)
                recv(t, piece, f"qy{s}{d}{h}")
                if d < 3 or h == "+-".index(s):
                    send(t, "y" + s, piece, f"qy{s}{d + 1}{h}")
                send(t, "p", piece, "p")

    def q4(t):
        for h, s in enumerate("+-"):
            piece = xrow(t, ys(4), h)
            recv(t, piece, f"qy{s}4{h}")
            send(t, "p", piece, "p")

    def g1(t):
        for h, (s, d) in enumerate((("+", -1), ("-", 1))):
            recv(t, ycol(t, xs(d)), "gx" + s)
            send(t, "x" + s, ycolhalf(t, xs(d), h), f"gx2{s}")
            send(t, "p", ycol(t, xs(d)), "p")

    def g2(t):
        for h, s in enumerate("+-"):
            piece = ycolhalf(t, xs(2), h)
            recv(t, piece, f"gx2{s}")
            send(t, "p", piece, "p")

    def pwait(t):
        recv(t, weights[t].at[:, :, 1 - c], "p")

    bins, width = cap_v.shape
    rows = img_v.shape[0]
    n_slots = out_buf.shape[0] * out_buf.shape[1]
    slot = out_buf.shape[1]

    def routing():
        owner = owner_ref[...]
        onehot_b = owner == lax.broadcasted_iota(jnp.int32, (bins, N_DP), 1)
        onehot = onehot_b.astype(F32)
        tri = (
            lax.broadcasted_iota(jnp.int32, (bins, bins), 1)
            < lax.broadcasted_iota(jnp.int32, (bins, bins), 0)
        ).astype(F32)
        before = jnp.dot(tri.astype(BF16), onehot.astype(BF16), preferred_element_type=F32)
        position = jnp.sum(before * onehot, axis=1, keepdims=True)
        target = owner * slot + position.astype(jnp.int32)
        picks[...] = (target == lax.broadcasted_iota(jnp.int32, (bins, n_slots), 1)).astype(F32).astype(BF16)
        counts = lax.dot_general(
            onehot.astype(BF16), jnp.ones((bins, 128), BF16), (((0,), (0,)), ((), ())),
            preferred_element_type=F32,
        )
        counts_out[...] = counts.reshape(N_DP, 1, 128)

    def split_mods():
        loads[2].wait()

        @pl.loop(0, width // 512)
        def _(i):
            cols = pl.ds(pl.multiple_of(i * 512, 512), 512)
            for j in (0, 1):
                value = cmod_v[:, j, cols]
                high = value.astype(BF16)
                rest = value - high.astype(F32)
                mid = rest.astype(BF16)
                low = (rest - mid.astype(F32)).astype(BF16)
                mod3[j, 0:N_DP, cols] = high
                mod3[j, N_DP : 2 * N_DP, cols] = mid
                mod3[j, 2 * N_DP :, cols] = low

    def row_mods():
        onehot = (owner_ref[...] == (lax.broadcasted_iota(jnp.int32, (bins, 3 * N_DP), 1) % N_DP)).astype(F32).astype(BF16)

        @pl.loop(0, width // 512)
        def _(i):
            cols = pl.ds(pl.multiple_of(i * 512, 512), 512)
            for j in (0, 1):
                modrow[j, :, cols] = jnp.dot(onehot, mod3[j, :, cols], preferred_element_type=F32)

    def norm(values):
        mean = jnp.mean(values, axis=-1, keepdims=True)
        values = values - mean
        var = jnp.mean(values * values, axis=-1, keepdims=True)
        return values * lax.rsqrt(var + 1e-06)

    def ln_txt(lo, n):
        @pl.loop(lo, lo + n)
        def _(i):
            r = pl.ds(pl.multiple_of(i * 16, 16), 16)
            values = norm(cap_v[r, :].astype(F32))
            txt_in[r, :] = (values * (1.0 + modrow[1, r, :]) + modrow[0, r, :]).astype(BF16)

    def ln_img(lo, n):
        @pl.loop(lo, lo + n)
        def _(i):
            r = pl.ds(pl.multiple_of(i * 16, 16), 16)
            values = norm(img_v[r, :].astype(F32))
            img_in[r, :] = (values * (1.0 + imod_ref[0, 1:2, :]) + imod_ref[0, 0:1, :]).astype(BF16)

    def project(left, t, p, gain_ref, n):
        total = None
        for xx in range(NX):
            w = weights[t][xx, :, :, p, :, :].reshape(width // NX, 256)
            part = jnp.dot(left[:, xx * (width // NX) : (xx + 1) * (width // NX)], w, preferred_element_type=F32)
            total = part if total is None else total + part
        if p == 2:
            return total.astype(BF16)
        heads = []
        for h in range(256 // HD):
            v = total[:, h * HD : (h + 1) * HD]
            v = v * lax.rsqrt(jnp.mean(v * v, axis=-1, keepdims=True) + 1e-06) * gain_ref[p : p + 1, :]
            heads.append(v)
        return jnp.concatenate(heads, axis=1).astype(BF16)

    def attend(blk, n):
        r = pl.ds(pl.multiple_of(blk * n, n), n)
        outs = []
        for h in range(256 // HD):
            lanes = slice(h * HD, (h + 1) * HD)
            s = lax.dot_general(
                qkv[0, r, lanes], qkv[1, :, lanes], (((1,), (1,)), ((), ())), preferred_element_type=F32
            )
            s = s + bias[0:1, :]
            top = jnp.max(s, axis=-1, keepdims=True)
            e = jnp.exp2((s - top) * (math.log2(math.e) / math.sqrt(HD)))
            e = e * (1.0 / jnp.sum(e, axis=-1, keepdims=True))
            outs.append(jnp.dot(e.astype(BF16), qkv[2, :, lanes], preferred_element_type=F32))
        return jnp.concatenate(outs, axis=1)

    def everyone(src, dst, k):
        own = pltpu.make_async_copy(src.at[dp], dst.at[dp], loc_sem.at[5 + k])
        own.start()

        @pl.loop(1, N_DP)
        def _(i):
            d = (dp + i) % N_DP
            pltpu.make_async_remote_copy(
                src_ref=src.at[d], dst_ref=dst.at[dp], send_sem=asem.at[0, k], recv_sem=asem.at[1, k],
                device_id={"dp": d}, device_id_type=MESH,
            ).start()

        def arrived():
            own.wait()
            pltpu.make_async_copy(dst.at[0 : N_DP - 1], dst.at[0 : N_DP - 1], asem.at[1, k]).wait()

        def left():
            pltpu.make_async_copy(src.at[0 : N_DP - 1], src.at[0 : N_DP - 1], asem.at[0, k]).wait()

        return arrived, left

    T, I = 0, 1
    loads[0].wait()
    loads[1].wait()
    pl.semaphore_wait(barrier, len(dev))
    s0(T)
    s0(I)
    routing()
    split_mods()
    r1(T)
    yphase(T, 1)
    xsend(T, -1, 1)
    yphase(I, 1)
    r1(I)
    r2(T)
    q0(T)
    row_mods()
    yphase(T, 2)
    xsend(T, -2, 2)
    xsend(I, -1, 1)
    r2(I)
    yphase(I, 2)
    loads[3].wait()
    ln_txt(0, 4)
    yphase(T, 3)
    xsend(T, -3, 3)
    qphase(T, 1)
    y4(T)
    xsend(T, 4)
    ln_txt(4, 4)
    yphase(I, 3)
    qphase(T, 2)
    ln_txt(8, 4)
    y4(I)
    q0(I)
    qphase(T, 3)
    ln_txt(12, 4)
    loads[4].wait()
    ln_img(0, 4)
    g1(T)
    xsend(I, -2, 2, -3, 3, 4)
    ln_img(4, 4)
    q4(T)
    g2(T)
    ln_img(8, 4)
    qphase(I, 1)
    pwait(T)
    counts_done, counts_left = everyone(counts_out, counts_in, 0)
    for p in range(3):
        payload[:, p * 256 : (p + 1) * 256] = project(txt_in, T, p, tgain_ref, bins)
        if p < 2:
            qphase(I, p + 2)
    for p in range(3):
        cols = slice(p * 256, (p + 1) * 256)
        routed = lax.dot_general(
            picks[...], payload[:, cols], (((0,), (0,)), ((), ())), preferred_element_type=F32
        )
        out_buf[:, :, cols] = routed.reshape(N_DP, slot, 256).astype(BF16)
    rows_done, rows_left = everyone(out_buf, in_buf, 1)
    q4(I)
    g1(I)
    ln_img(12, 20)
    g2(I)
    pwait(I)
    for p in range(3):
        qkv[p, n_slots:, :] = project(img_in, I, p, igain_ref, rows)
    counts_done()
    filled = counts_in[...].reshape(N_DP, 128)
    filled = jnp.concatenate([filled] * (n_slots // 128), axis=1)
    lane = lax.broadcasted_iota(jnp.int32, (N_DP, n_slots), 1)
    mine = lane // slot == lax.broadcasted_iota(jnp.int32, (N_DP, n_slots), 0)
    filled = jnp.sum(jnp.where(mine, filled, 0.0), axis=0, keepdims=True)
    place = (lax.broadcasted_iota(jnp.int32, (1, n_slots), 1) % slot).astype(F32)
    bias[0:1, 0:n_slots] = jnp.where(place < filled, 0.0, -jnp.inf)
    bias[0:1, n_slots:] = jnp.zeros((1, rows), F32)
    rows_done()
    for p in range(3):
        arrived = in_buf[:, :, p * 256 : (p + 1) * 256].astype(F32)
        qkv[p, 0:n_slots, :] = arrived.reshape(n_slots, 256).astype(BF16)
    n = 256

    @pl.loop(0, n_slots // n)
    def _(b):
        part = n // slot
        ret_out[pl.ds(b * part, part)] = attend(b, n).reshape(part, slot, 256).astype(BF16)

    back_done, back_left = everyone(ret_out, ret_in, 2)

    @pl.loop(0, rows // n)
    def _(b):
        oimg_ref[pl.ds(pl.multiple_of(b * n, n), n), :] = attend(n_slots // n + b, n).astype(BF16)

    back_done()
    returned = ret_in[...].astype(F32).reshape(n_slots, 256).astype(BF16)
    ocap_ref[...] = jnp.dot(picks[...], returned, preferred_element_type=F32).astype(BF16)
    for copy in sent:
        copy.wait_send()
    for left in (counts_left, rows_left, back_left):
        left()


def body(image_rows, image_mod, caption_rows, caption_mod, row_owner, w_img, w_txt, img_gain, txt_gain):
    rows, width = image_rows.shape
    bins = caption_rows.shape[0]
    slot = 2 * bins // N_DP
    n_slots = N_DP * slot
    depth, _, cols = w_img.shape
    w_img, w_txt = (jnp.transpose(w, (1, 0, 2)) for w in (w_img, w_txt))
    vmem = pl.BlockSpec(memory_space=pltpu.VMEM)
    hbm = pl.BlockSpec(memory_space=pl.ANY)
    return pl.pallas_call(
        kernel,
        out_shape=(
            jax.ShapeDtypeStruct((rows, cols), BF16),
            jax.ShapeDtypeStruct((bins, cols), BF16),
        ),
        in_specs=[hbm, vmem, hbm, hbm, vmem, hbm, hbm, vmem, vmem],
        out_specs=(vmem, vmem),
        scratch_shapes=[
            pltpu.VMEM((rows, width), BF16),
            pltpu.VMEM((bins, width), BF16),
            pltpu.VMEM((N_DP, 2, width), F32),
            pltpu.VMEM((2, 3 * N_DP, width), BF16),
            pltpu.VMEM((2, bins, width), F32),
            pltpu.VMEM((rows, width), BF16),
            pltpu.VMEM((bins, width), BF16),
            pltpu.VMEM((NX, NY, NC, 3, depth, cols), BF16),
            pltpu.VMEM((NX, NY, NC, 3, depth, cols), BF16),
            pltpu.VMEM((bins, n_slots), BF16),
            pltpu.VMEM((N_DP, 1, 128), F32),
            pltpu.VMEM((N_DP, 1, 128), F32),
            pltpu.VMEM((8, 128), F32),
            pltpu.VMEM((bins, 3 * cols), BF16),
            pltpu.VMEM((N_DP, slot, 3 * cols), BF16),
            pltpu.VMEM((N_DP, slot, 3 * cols), BF16),
            pltpu.VMEM((3, n_slots + rows, cols), BF16),
            pltpu.VMEM((N_DP, slot, cols), BF16),
            pltpu.VMEM((N_DP, slot, cols), BF16),
            pltpu.VMEM((8, n_slots + rows), F32),
            pltpu.SemaphoreType.DMA((8,)),
            pltpu.SemaphoreType.DMA((2, 32)),
            pltpu.SemaphoreType.DMA((2, 80)),
            pltpu.SemaphoreType.DMA((2, 3)),
        ],
        compiler_params=pltpu.CompilerParams(
            collective_id=0, has_side_effects=True, vmem_limit_bytes=60 * 1024 * 1024
        ),
        name="block",
    )(image_rows, image_mod, caption_rows, caption_mod, row_owner, w_img, w_txt, img_gain, txt_gain)


def solution(mesh):
    in_specs = (
        P("dp", None),
        P("dp", None, None),
        P("dp", None),
        P(),
        P("dp", None),
        P("dp", None, "tensor"),
        P("dp", None, "tensor"),
        P(),
        P(),
    )
    out_specs = (P("dp", "tensor"), P("dp", "tensor"))
    return jax.shard_map(body, mesh=mesh, in_specs=in_specs, out_specs=out_specs, check_vma=False)
```

```python
import math

import jax
import jax.numpy as jnp
from jax import lax
from jax.experimental import pallas as pl
from jax.experimental.pallas import tpu as pltpu
from jax.sharding import PartitionSpec as P

MESH = pl.DeviceIdType.MESH
HD = 128
NX, NY, NC = 4, 8, 2
N_DP = NX * NY * NC
F32 = jnp.float32
BF16 = jnp.bfloat16
T, I = 0, 1

ORDER = (
    ("s0", 0), ("s0", 1), ("route", 1), ("split", 8), ("rx", 0, "+"), ("rx", 0, "-"), ("split", 3), ("ry", 0, "+", 1),
    ("ry", 0, "-", 1), ("split", 1), ("mods", 2), ("gx", 0, "+", 0), ("gx", 0, "-", 0), ("qy", 0, 0, "+", 1),
    ("qy", 0, 0, "-", 1), ("mods", 10), ("rx", 1, "-"), ("gx", 1, "-", 0), ("lnt", 2), ("rx2", 0), ("qy", 0, -1, "+", 1),
    ("qy", 0, -1, "-", 1), ("lnt", 2), ("qy", 0, 1, "+", 1), ("qy", 0, 1, "-", 1), ("gx", 0, "-", -1), ("lnt", 2),
    ("gx", 0, "+", -1), ("lnt", 2), ("ry", 0, "+", 2), ("ry", 0, "-", 2), ("gx", 0, "-", 1), ("lnt", 2), ("gx", 0, "+", 1),
    ("qy", 0, 0, "+", 2), ("qy", 0, 0, "-", 2), ("lnt", 4), ("qy", 0, 2, "+", 1), ("qy", 0, 2, "-", 1), ("gx2", 0, "+", 0),
    ("lnt", 2), ("qy", 0, -1, "+", 2), ("qy", 0, -1, "-", 2), ("lni", 2), ("qy", 0, 1, "+", 2), ("qy", 0, 1, "-", 2),
    ("gx", 0, "-", -2), ("gx2", 0, "+", -1), ("gx", 1, "+", 0), ("lni", 4), ("ry", 0, "+", 3), ("ry", 0, "-", 3),
    ("gx", 0, "+", -2), ("gx", 0, "-", 2), ("lni", 2), ("qy", 0, 0, "+", 3), ("qy", 0, 0, "-", 3), ("qy", 1, 0, "-", 1),
    ("lni", 1), ("rx", 1, "+"), ("lni", 1), ("gx", 0, "+", 2), ("qy", 0, 2, "+", 2), ("qy", 0, 2, "-", 2),
    ("gx2", 0, "-", 1), ("lni", 1), ("qy", 0, -1, "+", 3), ("qy", 0, -1, "-", 3), ("lni", 2), ("qy", 0, 1, "+", 3),
    ("qy", 0, 1, "-", 3), ("gx2", 0, "-", -2), ("gx2", 1, "+", 0), ("lni", 2), ("ry", 0, "+", 4), ("ry", 0, "-", 4),
    ("qy", 1, 0, "+", 1), ("qy", 1, 1, "-", 1), ("lni", 1), ("rx2", 1), ("lni", 1), ("gx", 0, "+", -3), ("qy", 0, 0, "+", 4),
    ("gx", 0, "-", -3), ("lni", 1), ("qy", 1, 1, "+", 1), ("qy", 1, 0, "-", 2), ("lni", 2), ("gx", 0, "+", 3),
    ("qy", 0, 2, "+", 3), ("qy", 0, 2, "-", 3), ("gx", 0, "-", 3), ("qy", 1, -1, "+", 1), ("lni", 2), ("qy", 0, -1, "+", 4),
    ("qy", 0, 1, "-", 4), ("qy", 1, -1, "-", 1), ("lni", 2), ("gx2", 0, "+", 2), ("ry", 1, "+", 1), ("gx", 0, "-", 4),
    ("qy", 1, 1, "-", 2), ("lni", 1), ("qy", 1, 2, "-", 1), ("lni", 1), ("qy", 1, 0, "+", 2), ("lni", 1), ("gx", 0, "+", 4),
    ("qy", 1, 0, "-", 3), ("lni", 1), ("qy", 1, 2, "+", 1), ("lni", 1), ("qy", 0, 2, "-", 4), ("lni", 1), ("gx2", 0, "-", 3),
    ("ry", 1, "-", 1), ("qy", 1, 1, "+", 2), ("lni", 1), ("gx2", 0, "+", -3), ("lni", 1), ("qy", 1, -1, "+", 2),
    ("qy", 1, -1, "-", 2), ("ry", 1, "+", 2), ("gx", 1, "-", -1), ("qy", 1, 1, "-", 3), ("gx", 1, "+", -1),
    ("qy", 1, 2, "-", 2), ("qy", 1, 0, "+", 3), ("gx2", 0, "-", 4), ("qy", 1, 2, "+", 2), ("ry", 1, "-", 2),
    ("gx", 1, "+", 1), ("pw", 0), ("qy", 1, 1, "+", 3), ("gx", 1, "-", 1), ("qy", 1, -1, "+", 3), ("qy", 1, -1, "-", 3),
    ("proj", 0), ("gx", 1, "+", -2), ("qy", 1, 1, "-", 4), ("ry", 1, "+", 3), ("gx", 1, "-", -2), ("qy", 1, 2, "-", 3),
    ("send", 0, 0), ("send", 0, 1), ("qy", 1, 0, "+", 4), ("send", 0, 2), ("gx2", 1, "+", -1), ("qy", 1, 2, "+", 3),
    ("send", 0, 3), ("ry", 1, "-", 3), ("gx", 1, "-", 2), ("qy", 1, -1, "+", 4), ("send", 0, 4), ("gx", 1, "+", 2),
    ("ry", 1, "+", 4), ("qy", 1, 2, "-", 4), ("gx2", 1, "-", 1), ("send", 0, 5), ("gx", 1, "+", -3), ("send", 0, 6),
    ("gx", 1, "-", -3), ("gx2", 1, "-", -2), ("send", 0, 7), ("proj", 1), ("gx", 1, "+", 3), ("send", 1, 0),
    ("ry", 1, "-", 4), ("send", 1, 1), ("send", 1, 2), ("gx2", 1, "+", 2), ("send", 1, 3), ("gx", 1, "-", 3),
    ("gx2", 1, "+", -3), ("send", 1, 4), ("send", 1, 5), ("gx", 1, "-", 4), ("send", 1, 6), ("send", 1, 7), ("proj", 2),
    ("gx", 1, "+", 4), ("send", 2, 0), ("send", 2, 1), ("gx2", 1, "-", 3), ("send", 2, 2), ("send", 2, 3),
    ("gx2", 1, "-", 4), ("send", 2, 4), ("send", 2, 5), ("send", 2, 6), ("send", 2, 7), ("pw", 1),
)
ONWARD = {"+": (0, -1, 2, -3), "-": (1, -2, 3, 4)}


def sign(s):
    return 1 if s == "+" else -1


def kernel(
    img_hbm, imod_ref, cap_hbm, cmod_hbm, owner_ref, wimg_hbm, wtxt_hbm, igain_ref, tgain_ref,
    oimg_ref, ocap_ref,
    img_v, cap_v, cmod_v, mod3, modrow, img_in, txt_in, wt, wi, place_t, picks, onehot3, counts_out, counts_in,
    out_buf, in_buf, qkv, ret_out, ret_in, bias,
    loc_sem, rsem, ssem, asem,
):
    dp = lax.axis_index("dp")
    x, y, c = dp // (NY * NC), (dp // NC) % NY, dp % NC

    def at(xx, yy, cc):
        return (xx * NY + yy) * NC + cc

    def xs(d):
        return (x + d + NX) % NX

    def ys(d):
        return (y + d + NY) % NY

    dev = {
        "x+": at(xs(1), y, c), "x-": at(xs(-1), y, c),
        "y+": at(x, ys(1), c), "y-": at(x, ys(-1), c),
        "p": at(x, y, 1 - c),
    }
    weights = (wt, wi)

    loads = []
    for i, (src, dst) in enumerate((
        (wtxt_hbm, wt.at[x, y, c]), (wimg_hbm, wi.at[x, y, c]),
        (cmod_hbm, cmod_v), (cap_hbm, cap_v), (img_hbm, img_v),
    )):
        copy = pltpu.make_async_copy(src, dst, loc_sem.at[i])
        copy.start()
        loads.append(copy)

    barrier = pltpu.get_barrier_semaphore()
    for d in dev.values():
        pl.semaphore_signal(barrier, inc=1, device_id={"dp": d}, device_id_type=MESH)

    def ypiece(t, xx, yy):
        return weights[t].at[xx, yy, c, :, 16:48, :]

    def yhalf(t, xx, yy, s):
        lo = 16 if s == "+" else 32
        return weights[t].at[xx, yy, c, :, lo : lo + 16, :]

    def xpiece(t, xx, yy):
        return weights[t].at[xx, yy, c, :, 0:16, :]

    names = {}

    def sem(t, name):
        return rsem.at[t, names.setdefault(name, len(names))]

    def send(t, to, piece, name):
        kind = ("gx", "rx", "ry", "qy", "p").index("gx" if name[0] == "gx2" else "rx" if name[0] == "rx2" else name[0])
        pltpu.make_async_remote_copy(
            src_ref=piece, dst_ref=piece, send_sem=ssem.at[t, kind], recv_sem=sem(t, name),
            device_id={"dp": dev[to]}, device_id_type=MESH,
        ).start()

    def recv(t, piece, name):
        pltpu.make_async_copy(piece, piece, sem(t, name)).wait()

    def weights_sent(t):
        w = weights[t]
        for kind, piece in enumerate((
            w.at[0:2, :, 0], w.at[0, 0, 0], w.at[0:2, 0:7, 0, :, 0:16, :], w.at[:, 0:7, 0, :, 0:16, :], w.at[:, :, 0],
        )):
            pltpu.make_async_copy(piece, piece, ssem.at[t, kind]).wait()

    y4 = [0, 0]

    def s0(t):
        loads[t].wait()
        own_y, own_x = ypiece(t, x, y), xpiece(t, x, y)
        for s in "+-":
            send(t, "x" + s, own_x, ("rx", s))
            send(t, "y" + s, own_y, ("ry", s, 1))
            send(t, "x" + s, own_y, ("gx", s, 0))
        for s in "+-":
            send(t, "y" + s, own_x, ("qy", 0, s, 1))
        send(t, "p", weights[t].at[x, y, c], ("p",))

    def rx(t, s):
        piece = xpiece(t, xs(-sign(s)), y)
        recv(t, piece, ("rx", s))
        if s == "+-"[t]:
            send(t, "x" + s, piece, ("rx2",))
        for s2 in "+-":
            send(t, "y" + s2, piece, ("qy", -sign(s), s2, 1))
        send(t, "p", piece, ("p",))

    def rx2(t):
        piece = xpiece(t, xs(2), y)
        recv(t, piece, ("rx2",))
        for s2 in "+-":
            send(t, "y" + s2, piece, ("qy", 2, s2, 1))
        send(t, "p", piece, ("p",))

    def qy(t, j, s, d):
        piece = xpiece(t, xs(j), ys(-sign(s) * d))
        recv(t, piece, ("qy", j, s, d))
        if d < 3 or (d == 3 and (j in (0, -1)) == (s == "+")):
            send(t, "y" + s, piece, ("qy", j, s, d + 1))
        send(t, "p", piece, ("p",))

    def ry(t, s, d):
        if d == 4:
            piece = yhalf(t, x, ys(4), s)
            recv(t, piece, ("ry", s, 4))
            send(t, "p", piece, ("p",))
            y4[t] += 1
            if y4[t] == 2:
                for s2 in "+-":
                    send(t, "x" + s2, ypiece(t, x, ys(4)), ("gx", s2, 4))
            return
        dy = -sign(s) * d
        piece = ypiece(t, x, ys(dy))
        recv(t, piece, ("ry", s, d))
        if d < 3:
            send(t, "y" + s, piece, ("ry", s, d + 1))
        else:
            send(t, "y" + s, yhalf(t, x, ys(dy), s), ("ry", s, 4))
        for s2 in "+-":
            send(t, "x" + s2, piece, ("gx", s2, dy))
        send(t, "p", piece, ("p",))

    def gx(t, s, dy):
        piece = ypiece(t, xs(-sign(s)), ys(dy))
        recv(t, piece, ("gx", s, dy))
        if dy in ONWARD[s]:
            send(t, "x" + s, piece, ("gx2", s, dy))
        send(t, "p", piece, ("p",))

    def gx2(t, s, dy):
        piece = ypiece(t, xs(2), ys(dy))
        recv(t, piece, ("gx2", s, dy))
        send(t, "p", piece, ("p",))

    def pw(t):
        recv(t, weights[t].at[:, :, 1 - c], ("p",))

    bins, width = cap_v.shape
    rows = img_v.shape[0]
    _, _, slot, cols_dev = out_buf.shape
    n_slots = N_DP * slot
    iota = lambda shape, axis: lax.broadcasted_iota(jnp.int32, shape, axis)
    as_bf16 = lambda mask: mask.astype(F32).astype(BF16)

    def route():
        owner = owner_ref[...]
        own_t = as_bf16(owner == iota((N_DP, bins), 0))
        earlier = as_bf16(iota((bins, bins), 0) < iota((bins, bins), 1))
        before = jnp.dot(own_t, earlier, preferred_element_type=F32)
        position = jnp.sum(before * own_t.astype(F32), axis=0, keepdims=True)
        target = owner.astype(F32) * slot + position
        place_t[...] = as_bf16(iota((n_slots, bins), 0).astype(F32) == target)
        target_col = jnp.broadcast_to(target, (128, bins)).T[:, 0:1]
        picks[...] = as_bf16(iota((bins, n_slots), 1).astype(F32) == target_col)
        owner_col = jnp.broadcast_to(owner.astype(F32), (128, bins)).T[:, 0:1]
        onehot3[...] = as_bf16((iota((bins, 3 * N_DP), 1) % N_DP).astype(F32) == owner_col)
        counts = jnp.dot(own_t, jnp.ones((bins, 128), BF16), preferred_element_type=F32)
        counts_out[...] = counts.reshape(N_DP, 1, 128)

    tiles = width // 128

    def split(lo, n):
        @pl.loop(lo, lo + n)
        def _(k):
            lanes = pl.ds(pl.multiple_of(k * 128, 128), 128)
            for j in (0, 1):
                value = cmod_v[pl.ds(2 * k + j, N_DP, stride=2 * tiles), :]
                high = value.astype(BF16)
                rest = value - high.astype(F32)
                mid = rest.astype(BF16)
                low = (rest - mid.astype(F32)).astype(BF16)
                mod3[j, 0:N_DP, lanes] = high
                mod3[j, N_DP : 2 * N_DP, lanes] = mid
                mod3[j, 2 * N_DP :, lanes] = low

    def mods(lo, n):
        @pl.loop(lo, lo + n)
        def _(i):
            lanes = pl.ds(pl.multiple_of(i * 256, 256), 256)
            for j in (0, 1):
                modrow[j, :, lanes] = jnp.dot(onehot3[...], mod3[j, :, lanes], preferred_element_type=F32)

    def norm(values):
        values = values - jnp.mean(values, axis=-1, keepdims=True)
        var = jnp.mean(values * values, axis=-1, keepdims=True)
        return values * lax.rsqrt(var + 1e-06)

    def lnt(lo, n):
        @pl.loop(lo, lo + n)
        def _(i):
            r = pl.ds(pl.multiple_of(i * 16, 16), 16)
            values = norm(cap_v[r, :].astype(F32))
            txt_in[r, :] = (values * (1.0 + modrow[1, r, :]) + modrow[0, r, :]).astype(BF16)

    def lni(lo, n):
        @pl.loop(lo, lo + n)
        def _(i):
            r = pl.ds(pl.multiple_of(i * 16, 16), 16)
            values = norm(img_v[r, :].astype(F32))
            img_in[r, :] = (values * (1.0 + imod_ref[0, 1:2, :]) + imod_ref[0, 0:1, :]).astype(BF16)

    def project(left, t, p, gain_ref):
        total = None
        for xx in range(NX):
            w = weights[t][xx, :, :, p, :, :].reshape(width // NX, cols_dev)
            part = jnp.dot(left[:, xx * (width // NX) : (xx + 1) * (width // NX)], w, preferred_element_type=F32)
            total = part if total is None else total + part
        if p == 2:
            return total.astype(BF16)
        heads = []
        for h in range(cols_dev // HD):
            v = total[:, h * HD : (h + 1) * HD]
            v = v * lax.rsqrt(jnp.mean(v * v, axis=-1, keepdims=True) + 1e-06) * gain_ref[p : p + 1, :]
            heads.append(v)
        return jnp.concatenate(heads, axis=1).astype(BF16)

    def proj(p):
        routed = jnp.dot(place_t[...], project(txt_in, T, p, tgain_ref), preferred_element_type=F32)
        out_buf[p] = routed.reshape(N_DP, slot, cols_dev).astype(BF16)
        keep(out_buf.at[p], in_buf.at[p], 1 + p)

    kept = {}

    def keep(src, dst, k):
        kept[k] = (pltpu.make_async_copy(src.at[dp], dst.at[dp], loc_sem.at[5 + k]), src, dst)
        kept[k][0].start()

    def scatter(k, lo, hi):
        _, src, dst = kept[k]

        @pl.loop(lo, min(hi, N_DP - 1))
        def _(i):
            a, b, e = i // (NX * NC), (i // NC) % NX, i % NC
            dy = (4 - (a + 1) // 2) * (1 - 2 * ((a + 1) % 2))
            dx = (2 - (b + 1) // 2) * (1 - 2 * ((b + 1) % 2))
            d = at(xs(dx), ys(dy), (c + 1 + e) % NC)
            pltpu.make_async_remote_copy(
                src_ref=src.at[d], dst_ref=dst.at[dp], send_sem=asem.at[0, k], recv_sem=asem.at[1, k],
                device_id={"dp": d}, device_id_type=MESH,
            ).start()

    def arrived(k):
        own, _, dst = kept[k]
        own.wait()
        pltpu.make_async_copy(dst.at[0 : N_DP - 1], dst.at[0 : N_DP - 1], asem.at[1, k]).wait()

    def left(k):
        src = kept[k][1]
        pltpu.make_async_copy(src.at[0 : N_DP - 1], src.at[0 : N_DP - 1], asem.at[0, k]).wait()

    def attend(h, b, n):
        r = pl.ds(pl.multiple_of(b * n, n), n)
        lanes = slice(h * HD, (h + 1) * HD)
        s = lax.dot_general(
            qkv[0, r, lanes], qkv[1, :, lanes], (((1,), (1,)), ((), ())), preferred_element_type=F32
        )
        s = s + bias[0:1, :]
        top = jnp.max(s, axis=-1, keepdims=True)
        e = jnp.exp2((s - top) * (math.log2(math.e) / math.sqrt(HD)))
        e = e * (1.0 / jnp.sum(e, axis=-1, keepdims=True))
        return jnp.dot(e.astype(BF16), qkv[2, :, lanes], preferred_element_type=F32)

    pl.semaphore_wait(barrier, len(dev))
    moves = dict(s0=s0, rx=rx, rx2=rx2, qy=qy, ry=ry, gx=gx, gx2=gx2, pw=pw)
    work = dict(split=(split, 2, 2), mods=(mods, 1, None), lnt=(lnt, 1, 3), lni=(lni, 1, 4))
    done = dict.fromkeys(work, 0)
    for kind, *args in ORDER:
        if kind == "route":
            route()
        elif kind == "proj":
            proj(*args)
        elif kind == "send":
            p, batch = args
            scatter(1 + p, batch * NX * NC, (batch + 1) * NX * NC)
        elif kind in work:
            step, unit, load = work[kind]
            if load is not None and not done[kind]:
                loads[load].wait()
            step(done[kind] * unit, args[0] * unit)
            done[kind] += args[0]
        else:
            moves[kind](*args)
            if (kind, args[0]) == ("pw", T):
                keep(counts_out, counts_in, 0)
                scatter(0, 0, N_DP)
    for p in range(3):
        qkv[p, n_slots:, :] = project(img_in, I, p, igain_ref)
    arrived(0)
    filled = counts_in[...].reshape(N_DP, 128)
    filled = jnp.concatenate([filled] * (n_slots // 128), axis=1)
    mine = iota((N_DP, n_slots), 1) // slot == iota((N_DP, n_slots), 0)
    filled = jnp.sum(jnp.where(mine, filled, 0.0), axis=0, keepdims=True)
    place = (iota((1, n_slots), 1) % slot).astype(F32)
    bias[0:1, 0:n_slots] = jnp.where(place < filled, 0.0, -jnp.inf)
    bias[0:1, n_slots:] = jnp.zeros((1, rows), F32)
    for p in range(3):
        arrived(1 + p)
        qkv[p, 0:n_slots, :] = in_buf[p].astype(F32).reshape(n_slots, cols_dev).astype(BF16)
    n = 256
    part = n // slot
    heads = cols_dev // HD
    for h in range(heads):

        @pl.loop(0, n_slots // n)
        def _(b):
            ret_out[h, pl.ds(b * part, part)] = attend(h, b, n).reshape(part, slot, HD).astype(BF16)

        keep(ret_out.at[h], ret_in.at[h], 4 + h)
        scatter(4 + h, 0, N_DP)

    for h in range(heads):

        @pl.loop(0, rows // n)
        def _(b):
            lanes = slice(h * HD, (h + 1) * HD)
            oimg_ref[pl.ds(pl.multiple_of(b * n, n), n), lanes] = attend(h, n_slots // n + b, n).astype(BF16)

    weights_sent(T)
    weights_sent(I)
    for k in range(4 + heads):
        left(k)
    for h in range(heads):
        arrived(4 + h)
        returned = ret_in[h].astype(F32).reshape(n_slots, HD).astype(BF16)
        ocap_ref[:, h * HD : (h + 1) * HD] = jnp.dot(picks[...], returned, preferred_element_type=F32).astype(BF16)


def body(image_rows, image_mod, caption_rows, caption_mod, row_owner, w_img, w_txt, img_gain, txt_gain):
    rows, width = image_rows.shape
    bins = caption_rows.shape[0]
    slot = 2 * bins // N_DP
    n_slots = N_DP * slot
    depth, _, cols = w_img.shape
    w_img, w_txt = (jnp.transpose(w, (1, 0, 2)) for w in (w_img, w_txt))
    mods = caption_mod.reshape(N_DP, 2, width // 128, 128).transpose(0, 2, 1, 3).reshape(-1, 128)
    vmem = pl.BlockSpec(memory_space=pltpu.VMEM)
    hbm = pl.BlockSpec(memory_space=pl.ANY)
    return pl.pallas_call(
        kernel,
        out_shape=(
            jax.ShapeDtypeStruct((rows, cols), BF16),
            jax.ShapeDtypeStruct((bins, cols), BF16),
        ),
        in_specs=[hbm, vmem, hbm, hbm, vmem, hbm, hbm, vmem, vmem],
        out_specs=(vmem, vmem),
        scratch_shapes=[
            pltpu.VMEM((rows, width), BF16),
            pltpu.VMEM((bins, width), BF16),
            pltpu.VMEM(mods.shape, F32),
            pltpu.VMEM((2, 3 * N_DP, width), BF16),
            pltpu.VMEM((2, bins, width), F32),
            pltpu.VMEM((rows, width), BF16),
            pltpu.VMEM((bins, width), BF16),
            pltpu.VMEM((NX, NY, NC, 3, depth, cols), BF16),
            pltpu.VMEM((NX, NY, NC, 3, depth, cols), BF16),
            pltpu.VMEM((n_slots, bins), BF16),
            pltpu.VMEM((bins, n_slots), BF16),
            pltpu.VMEM((bins, 3 * N_DP), BF16),
            pltpu.VMEM((N_DP, 1, 128), F32),
            pltpu.VMEM((N_DP, 1, 128), F32),
            pltpu.VMEM((3, N_DP, slot, cols), BF16),
            pltpu.VMEM((3, N_DP, slot, cols), BF16),
            pltpu.VMEM((3, n_slots + rows, cols), BF16),
            pltpu.VMEM((cols // HD, N_DP, slot, HD), BF16),
            pltpu.VMEM((cols // HD, N_DP, slot, HD), BF16),
            pltpu.VMEM((8, n_slots + rows), F32),
            pltpu.SemaphoreType.DMA((16,)),
            pltpu.SemaphoreType.DMA((2, 64)),
            pltpu.SemaphoreType.DMA((2, 5)),
            pltpu.SemaphoreType.DMA((2, 6)),
        ],
        compiler_params=pltpu.CompilerParams(
            collective_id=0, has_side_effects=True, vmem_limit_bytes=60 * 1024 * 1024
        ),
        name="block",
    )(image_rows, image_mod, caption_rows, mods, row_owner.T, w_img, w_txt, img_gain, txt_gain)


def solution(mesh):
    in_specs = (
        P("dp", None),
        P("dp", None, None),
        P("dp", None),
        P(),
        P("dp", None),
        P("dp", None, "tensor"),
        P("dp", None, "tensor"),
        P(),
        P(),
    )
    out_specs = (P("dp", "tensor"), P("dp", "tensor"))
    return jax.shard_map(body, mesh=mesh, in_specs=in_specs, out_specs=out_specs, check_vma=False)
```

```python
import math

import jax
import jax.numpy as jnp
from jax import lax
from jax.experimental import pallas as pl
from jax.experimental.pallas import tpu as pltpu
from jax.sharding import PartitionSpec as P

MESH = pl.DeviceIdType.MESH
HD = 128
NX, NY, NC = 4, 8, 2
N_DP = NX * NY * NC
F32 = jnp.float32
BF16 = jnp.bfloat16
T, I = 0, 1

ORDER = (
    ("s0", 0), ("s0", 1), ("route", 1), ("split", 8), ("rx", 0, "+"), ("rx", 0, "-"), ("split", 3), ("ry", 0, "+", 1),
    ("ry", 0, "-", 1), ("split", 1), ("mods", 2), ("gx", 0, "+", 0), ("gx", 0, "-", 0), ("qy", 0, 0, "+", 1),
    ("qy", 0, 0, "-", 1), ("mods", 10), ("rx", 1, "-"), ("gx", 1, "-", 0), ("lnt", 2), ("rx2", 0), ("qy", 0, -1, "+", 1),
    ("qy", 0, -1, "-", 1), ("lnt", 2), ("qy", 0, 1, "+", 1), ("qy", 0, 1, "-", 1), ("gx", 0, "-", -1), ("lnt", 2),
    ("gx", 0, "+", -1), ("lnt", 2), ("ry", 0, "+", 2), ("ry", 0, "-", 2), ("gx", 0, "-", 1), ("lnt", 2), ("gx", 0, "+", 1),
    ("qy", 0, 0, "+", 2), ("qy", 0, 0, "-", 2), ("lnt", 4), ("qy", 0, 2, "+", 1), ("qy", 0, 2, "-", 1), ("gx2", 0, "+", 0),
    ("lnt", 2), ("qy", 0, -1, "+", 2), ("qy", 0, -1, "-", 2), ("lni", 2), ("qy", 0, 1, "+", 2), ("qy", 0, 1, "-", 2),
    ("gx", 0, "-", -2), ("gx2", 0, "+", -1), ("gx", 1, "+", 0), ("lni", 4), ("ry", 0, "+", 3), ("ry", 0, "-", 3),
    ("gx", 0, "+", -2), ("gx", 0, "-", 2), ("lni", 2), ("qy", 0, 0, "+", 3), ("qy", 0, 0, "-", 3), ("qy", 1, 0, "-", 1),
    ("lni", 1), ("rx", 1, "+"), ("lni", 1), ("gx", 0, "+", 2), ("qy", 0, 2, "+", 2), ("qy", 0, 2, "-", 2),
    ("gx2", 0, "-", 1), ("lni", 1), ("qy", 0, -1, "+", 3), ("qy", 0, -1, "-", 3), ("lni", 2), ("qy", 0, 1, "+", 3),
    ("qy", 0, 1, "-", 3), ("gx2", 0, "-", -2), ("gx2", 1, "+", 0), ("lni", 2), ("ry", 0, "+", 4), ("ry", 0, "-", 4),
    ("qy", 1, 0, "+", 1), ("qy", 1, 1, "-", 1), ("lni", 1), ("rx2", 1), ("lni", 1), ("gx", 0, "+", -3), ("qy", 0, 0, "+", 4),
    ("gx", 0, "-", -3), ("lni", 1), ("qy", 1, 1, "+", 1), ("qy", 1, 0, "-", 2), ("lni", 2), ("gx", 0, "+", 3),
    ("qy", 0, 2, "+", 3), ("qy", 0, 2, "-", 3), ("gx", 0, "-", 3), ("qy", 1, -1, "+", 1), ("lni", 2), ("qy", 0, -1, "+", 4),
    ("qy", 0, 1, "-", 4), ("qy", 1, -1, "-", 1), ("lni", 2), ("gx2", 0, "+", 2), ("ry", 1, "+", 1), ("gx", 0, "-", 4),
    ("qy", 1, 1, "-", 2), ("lni", 1), ("qy", 1, 2, "-", 1), ("lni", 1), ("qy", 1, 0, "+", 2), ("lni", 1), ("gx", 0, "+", 4),
    ("qy", 1, 0, "-", 3), ("lni", 1), ("qy", 1, 2, "+", 1), ("lni", 1), ("qy", 0, 2, "-", 4), ("lni", 1), ("gx2", 0, "-", 3),
    ("ry", 1, "-", 1), ("qy", 1, 1, "+", 2), ("lni", 1), ("gx2", 0, "+", -3), ("lni", 1), ("qy", 1, -1, "+", 2),
    ("qy", 1, -1, "-", 2), ("ry", 1, "+", 2), ("gx", 1, "-", -1), ("qy", 1, 1, "-", 3), ("gx", 1, "+", -1),
    ("qy", 1, 2, "-", 2), ("qy", 1, 0, "+", 3), ("gx2", 0, "-", 4), ("qy", 1, 2, "+", 2), ("ry", 1, "-", 2),
    ("gx", 1, "+", 1), ("pw", 0), ("qy", 1, 1, "+", 3), ("gx", 1, "-", 1), ("qy", 1, -1, "+", 3), ("qy", 1, -1, "-", 3),
    ("proj", 0), ("gx", 1, "+", -2), ("qy", 1, 1, "-", 4), ("ry", 1, "+", 3), ("gx", 1, "-", -2), ("qy", 1, 2, "-", 3),
    ("send", 0, 0), ("send", 0, 1), ("qy", 1, 0, "+", 4), ("send", 0, 2), ("gx2", 1, "+", -1), ("qy", 1, 2, "+", 3),
    ("send", 0, 3), ("ry", 1, "-", 3), ("gx", 1, "-", 2), ("qy", 1, -1, "+", 4), ("send", 0, 4), ("gx", 1, "+", 2),
    ("ry", 1, "+", 4), ("qy", 1, 2, "-", 4), ("gx2", 1, "-", 1), ("send", 0, 5), ("gx", 1, "+", -3), ("send", 0, 6),
    ("gx", 1, "-", -3), ("gx2", 1, "-", -2), ("send", 0, 7), ("proj", 1), ("gx", 1, "+", 3), ("send", 1, 0),
    ("ry", 1, "-", 4), ("send", 1, 1), ("send", 1, 2), ("gx2", 1, "+", 2), ("send", 1, 3), ("gx", 1, "-", 3),
    ("gx2", 1, "+", -3), ("send", 1, 4), ("send", 1, 5), ("gx", 1, "-", 4), ("send", 1, 6), ("send", 1, 7), ("proj", 2),
    ("gx", 1, "+", 4), ("send", 2, 0), ("send", 2, 1), ("gx2", 1, "-", 3), ("send", 2, 2), ("send", 2, 3),
    ("gx2", 1, "-", 4), ("send", 2, 4), ("send", 2, 5), ("send", 2, 6), ("send", 2, 7), ("pw", 1),
)
ONWARD = {"+": (0, -1, 2, -3), "-": (1, -2, 3, 4)}


def sign(s):
    return 1 if s == "+" else -1


def kernel(
    img_hbm, imod_ref, cap_hbm, cmod_hbm, owner_ref, wimg_hbm, wtxt_hbm, igain_ref, tgain_ref,
    oimg_ref, ocap_ref,
    img_v, cap_v, cmod_v, mod3, modrow, img_in, txt_in, wt, wi, place_t, picks, onehot3, counts_out, counts_in,
    out_buf, in_buf, qkv, ret_out, ret_in, bias,
    loc_sem, rsem, ssem, asem,
):
    dp = lax.axis_index("dp")
    x, y, c = dp // (NY * NC), (dp // NC) % NY, dp % NC

    def at(xx, yy, cc):
        return (xx * NY + yy) * NC + cc

    def xs(d):
        return (x + d + NX) % NX

    def ys(d):
        return (y + d + NY) % NY

    dev = {
        "x+": at(xs(1), y, c), "x-": at(xs(-1), y, c),
        "y+": at(x, ys(1), c), "y-": at(x, ys(-1), c),
        "p": at(x, y, 1 - c),
    }
    weights = (wt, wi)

    loads = []
    for i, (src, dst) in enumerate((
        (wtxt_hbm, wt.at[x, y, c]), (wimg_hbm, wi.at[x, y, c]),
        (cmod_hbm, cmod_v), (cap_hbm, cap_v), (img_hbm, img_v),
    )):
        copy = pltpu.make_async_copy(src, dst, loc_sem.at[i])
        copy.start()
        loads.append(copy)

    barrier = pltpu.get_barrier_semaphore()
    for d in dev.values():
        pl.semaphore_signal(barrier, inc=1, device_id={"dp": d}, device_id_type=MESH)

    def ypiece(t, xx, yy):
        return weights[t].at[xx, yy, c, :, 16:48, :]

    def yhalf(t, xx, yy, s):
        lo = 16 if s == "+" else 32
        return weights[t].at[xx, yy, c, :, lo : lo + 16, :]

    def xpiece(t, xx, yy):
        return weights[t].at[xx, yy, c, :, 0:16, :]

    names = {}

    def sem(t, name):
        return rsem.at[t, names.setdefault(name, len(names))]

    def send(t, to, piece, name, source=None):
        kind = ("gx", "rx", "ry", "qy", "p").index("gx" if name[0] == "gx2" else "rx" if name[0] == "rx2" else name[0])
        pltpu.make_async_remote_copy(
            src_ref=piece if source is None else source, dst_ref=piece, send_sem=ssem.at[t, kind], recv_sem=sem(t, name),
            device_id={"dp": dev[to]}, device_id_type=MESH,
        ).start()

    def recv(t, piece, name):
        pltpu.make_async_copy(piece, piece, sem(t, name)).wait()

    def weights_sent(t):
        w = weights[t]
        for kind, piece in enumerate((
            w.at[0:2, :, 0], w.at[0, 0, 0], w.at[0:2, 0:7, 0, :, 0:16, :], w.at[:, 0:7, 0, :, 0:16, :], w.at[:, :, 0],
        )):
            pltpu.make_async_copy(piece, piece, ssem.at[t, kind]).wait()

    y4 = [0, 0]

    def s0(t):
        shard = (wtxt_hbm, wimg_hbm)[t]
        own_y, own_x = ypiece(t, x, y), xpiece(t, x, y)
        from_y, from_x = shard.at[:, 16:48, :], shard.at[:, 0:16, :]
        for s in "+-":
            send(t, "x" + s, own_x, ("rx", s), from_x)
            send(t, "y" + s, own_y, ("ry", s, 1), from_y)
            send(t, "x" + s, own_y, ("gx", s, 0), from_y)
        for s in "+-":
            send(t, "y" + s, own_x, ("qy", 0, s, 1), from_x)
        send(t, "p", weights[t].at[x, y, c], ("p",), shard)

    def rx(t, s):
        piece = xpiece(t, xs(-sign(s)), y)
        recv(t, piece, ("rx", s))
        send(t, "p", piece, ("p",))
        if s == "+-"[t]:
            send(t, "x" + s, piece, ("rx2",))
        for s2 in "+-":
            send(t, "y" + s2, piece, ("qy", -sign(s), s2, 1))

    def rx2(t):
        piece = xpiece(t, xs(2), y)
        recv(t, piece, ("rx2",))
        send(t, "p", piece, ("p",))
        for s2 in "+-":
            send(t, "y" + s2, piece, ("qy", 2, s2, 1))

    def qy(t, j, s, d):
        piece = xpiece(t, xs(j), ys(-sign(s) * d))
        recv(t, piece, ("qy", j, s, d))
        send(t, "p", piece, ("p",))
        if d < 3 or (d == 3 and (j in (0, -1)) == (s == "+")):
            send(t, "y" + s, piece, ("qy", j, s, d + 1))

    def ry(t, s, d):
        if d == 4:
            piece = yhalf(t, x, ys(4), s)
            recv(t, piece, ("ry", s, 4))
            send(t, "p", piece, ("p",))
            y4[t] += 1
            if y4[t] == 2:
                for s2 in "+-":
                    send(t, "x" + s2, ypiece(t, x, ys(4)), ("gx", s2, 4))
            return
        dy = -sign(s) * d
        piece = ypiece(t, x, ys(dy))
        recv(t, piece, ("ry", s, d))
        send(t, "p", piece, ("p",))
        if d < 3:
            send(t, "y" + s, piece, ("ry", s, d + 1))
        else:
            send(t, "y" + s, yhalf(t, x, ys(dy), s), ("ry", s, 4))
        for s2 in "+-":
            send(t, "x" + s2, piece, ("gx", s2, dy))

    def gx(t, s, dy):
        piece = ypiece(t, xs(-sign(s)), ys(dy))
        recv(t, piece, ("gx", s, dy))
        send(t, "p", piece, ("p",))
        if dy in ONWARD[s]:
            send(t, "x" + s, piece, ("gx2", s, dy))

    def gx2(t, s, dy):
        piece = ypiece(t, xs(2), ys(dy))
        recv(t, piece, ("gx2", s, dy))
        send(t, "p", piece, ("p",))

    def pw(t):
        recv(t, weights[t].at[:, :, 1 - c], ("p",))
        loads[t].wait()

    bins, width = cap_v.shape
    rows = img_v.shape[0]
    _, _, slot, cols_dev = out_buf.shape
    n_slots = N_DP * slot
    iota = lambda shape, axis: lax.broadcasted_iota(jnp.int32, shape, axis)
    as_bf16 = lambda mask: mask.astype(F32).astype(BF16)

    def route():
        owner = owner_ref[...]
        own_t = as_bf16(owner == iota((N_DP, bins), 0))
        earlier = as_bf16(iota((bins, bins), 0) < iota((bins, bins), 1))
        before = jnp.dot(own_t, earlier, preferred_element_type=F32)
        position = jnp.sum(before * own_t.astype(F32), axis=0, keepdims=True)
        target = owner.astype(F32) * slot + position
        place_t[...] = as_bf16(iota((n_slots, bins), 0).astype(F32) == target)
        target_col = jnp.broadcast_to(target, (128, bins)).T[:, 0:1]
        picks[...] = as_bf16(iota((bins, n_slots), 1).astype(F32) == target_col)
        owner_col = jnp.broadcast_to(owner.astype(F32), (128, bins)).T[:, 0:1]
        onehot3[...] = as_bf16((iota((bins, 3 * N_DP), 1) % N_DP).astype(F32) == owner_col)
        counts = jnp.dot(own_t, jnp.ones((bins, 128), BF16), preferred_element_type=F32)
        counts_out[...] = counts.reshape(N_DP, 1, 128)

    tiles = width // 128

    def split(lo, n):
        @pl.loop(lo, lo + n)
        def _(k):
            lanes = pl.ds(pl.multiple_of(k * 128, 128), 128)
            for j in (0, 1):
                value = cmod_v[pl.ds(2 * k + j, N_DP, stride=2 * tiles), :]
                high = value.astype(BF16)
                rest = value - high.astype(F32)
                mid = rest.astype(BF16)
                low = (rest - mid.astype(F32)).astype(BF16)
                mod3[j, 0:N_DP, lanes] = high
                mod3[j, N_DP : 2 * N_DP, lanes] = mid
                mod3[j, 2 * N_DP :, lanes] = low

    def mods(lo, n):
        @pl.loop(lo, lo + n)
        def _(i):
            lanes = pl.ds(pl.multiple_of(i * 256, 256), 256)
            for j in (0, 1):
                modrow[j, :, lanes] = jnp.dot(onehot3[...], mod3[j, :, lanes], preferred_element_type=F32)

    def norm(values):
        values = values - jnp.mean(values, axis=-1, keepdims=True)
        var = jnp.mean(values * values, axis=-1, keepdims=True)
        return values * lax.rsqrt(var + 1e-06)

    def lnt(lo, n):
        @pl.loop(lo, lo + n)
        def _(i):
            r = pl.ds(pl.multiple_of(i * 16, 16), 16)
            values = norm(cap_v[r, :].astype(F32))
            txt_in[r, :] = (values * (1.0 + modrow[1, r, :]) + modrow[0, r, :]).astype(BF16)

    def lni(lo, n):
        @pl.loop(lo, lo + n)
        def _(i):
            r = pl.ds(pl.multiple_of(i * 16, 16), 16)
            values = norm(img_v[r, :].astype(F32))
            img_in[r, :] = (values * (1.0 + imod_ref[0, 1:2, :]) + imod_ref[0, 0:1, :]).astype(BF16)

    def project(left, t, p, gain_ref):
        total = None
        for xx in range(NX):
            w = weights[t][xx, :, :, p, :, :].reshape(width // NX, cols_dev)
            part = jnp.dot(left[:, xx * (width // NX) : (xx + 1) * (width // NX)], w, preferred_element_type=F32)
            total = part if total is None else total + part
        if p == 2:
            return total.astype(BF16)
        heads = []
        for h in range(cols_dev // HD):
            v = total[:, h * HD : (h + 1) * HD]
            v = v * lax.rsqrt(jnp.mean(v * v, axis=-1, keepdims=True) + 1e-06) * gain_ref[p : p + 1, :]
            heads.append(v)
        return jnp.concatenate(heads, axis=1).astype(BF16)

    def proj(p):
        routed = jnp.dot(place_t[...], project(txt_in, T, p, tgain_ref), preferred_element_type=F32)
        out_buf[p] = routed.reshape(N_DP, slot, cols_dev).astype(BF16)
        keep(out_buf.at[p], in_buf.at[p], 1 + p)

    kept = {}

    def keep(src, dst, k):
        kept[k] = (pltpu.make_async_copy(src.at[dp], dst.at[dp], loc_sem.at[5 + k]), src, dst)
        kept[k][0].start()

    xnear = [xs(dx) * NY for dx in (2, 1, -1, 0)]
    cnear = [1 - c, c]

    def ring(k, yy, n):
        _, src, dst = kept[k]
        for i in range(n):
            d = (xnear[i // NC] + yy) * NC + cnear[i % NC]
            pltpu.make_async_remote_copy(
                src_ref=src.at[d], dst_ref=dst.at[dp], send_sem=asem.at[0, k], recv_sem=asem.at[1, k],
                device_id={"dp": d}, device_id_type=MESH,
            ).start()

    def scatter(k):
        @pl.loop(0, NY - 1)
        def _(a):
            ring(k, ys((4 - (a + 1) // 2) * (1 - 2 * ((a + 1) % 2))), NX * NC)

        ring(k, y, NX * NC - 1)

    def arrived(k):
        own, _, dst = kept[k]
        own.wait()
        pltpu.make_async_copy(dst.at[0 : N_DP - 1], dst.at[0 : N_DP - 1], asem.at[1, k]).wait()

    def left(k):
        src = kept[k][1]
        pltpu.make_async_copy(src.at[0 : N_DP - 1], src.at[0 : N_DP - 1], asem.at[0, k]).wait()

    def attend(h, b, n):
        r = pl.ds(pl.multiple_of(b * n, n), n)
        lanes = slice(h * HD, (h + 1) * HD)
        s = lax.dot_general(
            qkv[0, r, lanes], qkv[1, :, lanes], (((1,), (1,)), ((), ())), preferred_element_type=F32
        )
        s = s + bias[0:1, :]
        top = jnp.max(s, axis=-1, keepdims=True)
        e = jnp.exp2((s - top) * (math.log2(math.e) / math.sqrt(HD)))
        out = jnp.dot(e.astype(BF16), qkv[2, :, lanes], preferred_element_type=F32)
        return out * (1.0 / jnp.sum(e, axis=-1, keepdims=True))

    pl.semaphore_wait(barrier, len(dev))
    moves = dict(s0=s0, rx=rx, rx2=rx2, qy=qy, ry=ry, gx=gx, gx2=gx2, pw=pw)
    work = dict(split=(split, 2, 2), mods=(mods, 1, None), lnt=(lnt, 1, 3), lni=(lni, 1, 4))
    done = dict.fromkeys(work, 0)
    for kind, *args in ORDER:
        if kind == "route":
            route()
        elif kind == "proj":
            proj(*args)
        elif kind == "send":
            p, batch = args
            ring(1 + p, ys((4, 3, -3, 2, -2, 1, -1, 0)[batch]), NX * NC - (batch == NY - 1))
        elif kind in work:
            step, unit, load = work[kind]
            if load is not None and not done[kind]:
                loads[load].wait()
            step(done[kind] * unit, args[0] * unit)
            done[kind] += args[0]
        else:
            moves[kind](*args)
    keep(counts_out, counts_in, 0)
    scatter(0)
    for p in range(3):
        qkv[p, n_slots:, :] = project(img_in, I, p, igain_ref)
    arrived(0)
    filled = counts_in[...].reshape(N_DP, 128)
    filled = jnp.concatenate([filled] * (n_slots // 128), axis=1)
    mine = iota((N_DP, n_slots), 1) // slot == iota((N_DP, n_slots), 0)
    filled = jnp.sum(jnp.where(mine, filled, 0.0), axis=0, keepdims=True)
    place = (iota((1, n_slots), 1) % slot).astype(F32)
    bias[0:1, 0:n_slots] = jnp.where(place < filled, 0.0, -jnp.inf)
    bias[0:1, n_slots:] = jnp.zeros((1, rows), F32)
    for p in range(3):
        arrived(1 + p)
        qkv[p, 0:n_slots, :] = in_buf[p].astype(F32).reshape(n_slots, cols_dev).astype(BF16)
    n = 256
    part = n // slot
    heads = cols_dev // HD
    for h in range(heads):

        @pl.loop(0, n_slots // n)
        def _(b):
            ret_out[h, pl.ds(b * part, part)] = attend(h, b, n).reshape(part, slot, HD).astype(BF16)

        keep(ret_out.at[h], ret_in.at[h], 4 + h)
        scatter(4 + h)

    for h in range(heads):

        @pl.loop(0, rows // n)
        def _(b):
            lanes = slice(h * HD, (h + 1) * HD)
            oimg_ref[pl.ds(pl.multiple_of(b * n, n), n), lanes] = attend(h, n_slots // n + b, n).astype(BF16)

    weights_sent(T)
    weights_sent(I)
    for k in range(4 + heads):
        left(k)
    for h in range(heads):
        arrived(4 + h)
        returned = ret_in[h].astype(F32).reshape(n_slots, HD).astype(BF16)
        ocap_ref[:, h * HD : (h + 1) * HD] = jnp.dot(picks[...], returned, preferred_element_type=F32).astype(BF16)


def finish(image_ref, caption_ref, oimg_ref, ocap_ref):
    oimg_ref[...] = image_ref[...]
    ocap_ref[...] = caption_ref[...]


def body(image_rows, image_mod, caption_rows, caption_mod, row_owner, w_img, w_txt, img_gain, txt_gain):
    rows, width = image_rows.shape
    bins = caption_rows.shape[0]
    slot = 2 * bins // N_DP
    n_slots = N_DP * slot
    depth, _, cols = w_img.shape
    w_img, w_txt = (jnp.transpose(w, (1, 0, 2)) for w in (w_img, w_txt))
    mods = caption_mod.reshape(N_DP, 2, width // 128, 128).transpose(0, 2, 1, 3).reshape(-1, 128)
    vmem = pl.BlockSpec(memory_space=pltpu.VMEM)
    hbm = pl.BlockSpec(memory_space=pl.ANY)
    outs = pl.pallas_call(
        kernel,
        out_shape=(
            jax.ShapeDtypeStruct((rows, cols), BF16),
            jax.ShapeDtypeStruct((bins, cols), BF16),
        ),
        in_specs=[hbm, vmem, hbm, hbm, vmem, hbm, hbm, vmem, vmem],
        out_specs=(vmem, vmem),
        scratch_shapes=[
            pltpu.VMEM((rows, width), BF16),
            pltpu.VMEM((bins, width), BF16),
            pltpu.VMEM(mods.shape, F32),
            pltpu.VMEM((2, 3 * N_DP, width), BF16),
            pltpu.VMEM((2, bins, width), F32),
            pltpu.VMEM((rows, width), BF16),
            pltpu.VMEM((bins, width), BF16),
            pltpu.VMEM((NX, NY, NC, 3, depth, cols), BF16),
            pltpu.VMEM((NX, NY, NC, 3, depth, cols), BF16),
            pltpu.VMEM((n_slots, bins), BF16),
            pltpu.VMEM((bins, n_slots), BF16),
            pltpu.VMEM((bins, 3 * N_DP), BF16),
            pltpu.VMEM((N_DP, 1, 128), F32),
            pltpu.VMEM((N_DP, 1, 128), F32),
            pltpu.VMEM((3, N_DP, slot, cols), BF16),
            pltpu.VMEM((3, N_DP, slot, cols), BF16),
            pltpu.VMEM((3, n_slots + rows, cols), BF16),
            pltpu.VMEM((cols // HD, N_DP, slot, HD), BF16),
            pltpu.VMEM((cols // HD, N_DP, slot, HD), BF16),
            pltpu.VMEM((8, n_slots + rows), F32),
            pltpu.SemaphoreType.DMA((16,)),
            pltpu.SemaphoreType.DMA((2, 64)),
            pltpu.SemaphoreType.DMA((2, 5)),
            pltpu.SemaphoreType.DMA((2, 6)),
        ],
        compiler_params=pltpu.CompilerParams(
            collective_id=0, has_side_effects=True, vmem_limit_bytes=60 * 1024 * 1024
        ),
        name="block",
    )(image_rows, image_mod, caption_rows, mods, row_owner.T, w_img, w_txt, img_gain, txt_gain)
    return pl.pallas_call(
        finish,
        out_shape=tuple(jax.ShapeDtypeStruct(o.shape, o.dtype) for o in outs),
        in_specs=[vmem, vmem],
        out_specs=(vmem, vmem),
        compiler_params=pltpu.CompilerParams(vmem_limit_bytes=4 * 1024 * 1024),
        name="finish",
    )(*outs)


def solution(mesh):
    in_specs = (
        P("dp", None),
        P("dp", None, None),
        P("dp", None),
        P(),
        P("dp", None),
        P("dp", None, "tensor"),
        P("dp", None, "tensor"),
        P(),
        P(),
    )
    out_specs = (P("dp", "tensor"), P("dp", "tensor"))
    return jax.shard_map(body, mesh=mesh, in_specs=in_specs, out_specs=out_specs, check_vma=False)
```

```python
import math

import jax
import jax.numpy as jnp
from jax import lax
from jax.experimental import pallas as pl
from jax.experimental.pallas import tpu as pltpu
from jax.sharding import PartitionSpec as P

MESH = pl.DeviceIdType.MESH
HD = 128
NX, NY, NC = 4, 8, 2
N_DP = NX * NY * NC
F32 = jnp.float32
BF16 = jnp.bfloat16
T, I = 0, 1

ORDER = (
    ("s0", 0), ("s0", 1), ("route", 1), ("split", 10), ("rx", 0, "+"), ("rx", 0, "-"), ("split", 2), ("mods", 1),
    ("ry", 0, "+", 1), ("ry", 0, "-", 1), ("mods", 3), ("gx", 0, "+", 0), ("gx", 0, "-", 0), ("qy", 0, 0, "+", 1),
    ("qy", 0, 0, "-", 1), ("mods", 3), ("rx", 1, "-"), ("mods", 5), ("lnt", 1), ("gx", 1, "-", 0), ("rx", 1, "+"),
    ("lnt", 2), ("rx2", 0), ("qy", 0, -1, "+", 1), ("qy", 0, -1, "-", 1), ("gx", 1, "+", 0), ("lnt", 2),
    ("qy", 0, 1, "+", 1), ("qy", 0, 1, "-", 1), ("gx", 0, "-", -1), ("lnt", 2), ("gx", 0, "+", -1), ("lnt", 2),
    ("ry", 0, "+", 2), ("ry", 0, "-", 2), ("gx", 0, "-", 1), ("lnt", 2), ("gx", 0, "+", 1), ("qy", 0, 0, "+", 2),
    ("qy", 0, 0, "-", 2), ("lnt", 4), ("gx2", 0, "+", 0), ("qy", 1, 0, "+", 1), ("qy", 1, 0, "-", 1), ("lnt", 1), ("lni", 1),
    ("qy", 0, 2, "+", 1), ("qy", 0, 2, "-", 1), ("lni", 2), ("qy", 0, -1, "+", 2), ("qy", 0, -1, "-", 2), ("gx2", 1, "+", 0),
    ("lni", 1), ("gx", 0, "-", -2), ("qy", 0, 1, "+", 2), ("qy", 0, 1, "-", 2), ("lni", 2), ("gx2", 0, "+", -1),
    ("ry", 1, "+", 1), ("qy", 1, 1, "-", 1), ("lni", 2), ("ry", 0, "+", 3), ("ry", 0, "-", 3), ("gx", 0, "-", 2), ("lni", 2),
    ("gx", 0, "+", -2), ("qy", 0, 0, "+", 3), ("qy", 0, 0, "-", 3), ("qy", 1, -1, "-", 1), ("lni", 2), ("gx2", 0, "-", 1),
    ("qy", 1, 0, "-", 2), ("lni", 2), ("gx", 0, "+", 2), ("qy", 0, 2, "+", 2), ("qy", 0, 2, "-", 2), ("lni", 1),
    ("gx2", 0, "-", -2), ("qy", 0, -1, "+", 3), ("qy", 0, -1, "-", 3), ("lni", 2), ("qy", 0, 1, "+", 3),
    ("qy", 0, 1, "-", 3), ("ry", 1, "-", 1), ("qy", 1, 1, "+", 1), ("lni", 2), ("qy", 1, -1, "+", 1), ("gx", 1, "-", -1),
    ("lni", 2), ("ry", 0, "-", 4), ("gx", 0, "+", -3), ("rx2", 1), ("lni", 2), ("ry", 0, "+", 4), ("gx", 0, "-", -3),
    ("qy", 1, 0, "+", 2), ("qy", 1, 1, "-", 2), ("lni", 2), ("gx", 0, "+", 3), ("qy", 0, 0, "+", 4), ("qy", 1, -1, "-", 2),
    ("lni", 1), ("gx", 0, "-", 3), ("qy", 0, 2, "+", 3), ("qy", 0, 2, "-", 3), ("lni", 2), ("qy", 0, -1, "+", 4),
    ("qy", 0, 1, "-", 4), ("gx2", 0, "+", 2), ("gx", 1, "+", -1), ("qy", 1, 0, "-", 3), ("lni", 2), ("gx", 1, "-", 1),
    ("qy", 1, 1, "+", 2), ("lni", 2), ("ry", 1, "+", 2), ("gx", 1, "+", 1), ("qy", 1, -1, "+", 2), ("gx", 0, "-", 4),
    ("qy", 1, 2, "-", 1), ("qy", 1, 2, "+", 1), ("gx2", 0, "+", -3), ("qy", 1, 1, "-", 3), ("qy", 1, 0, "+", 3),
    ("gx2", 0, "-", 3), ("ry", 1, "-", 2), ("qy", 1, -1, "-", 3), ("gx", 0, "+", 4), ("qy", 0, 2, "-", 4),
    ("qy", 1, 1, "+", 3), ("gx2", 1, "-", 1), ("qy", 1, 2, "-", 2), ("gx2", 1, "+", -1), ("ry", 1, "+", 3),
    ("qy", 1, 1, "-", 4), ("qy", 1, -1, "+", 3), ("gx", 1, "-", -2), ("gx", 1, "+", -2), ("qy", 1, 2, "+", 2),
    ("gx2", 0, "-", 4), ("ry", 1, "-", 3), ("qy", 1, 0, "+", 4), ("gx", 1, "+", 2), ("qy", 1, 2, "-", 3), ("gx", 1, "-", 2),
    ("ry", 1, "+", 4), ("pw", 0), ("proj", 0), ("qy", 1, -1, "+", 4), ("gx", 1, "+", -3), ("qy", 1, 2, "+", 3),
    ("gx", 1, "-", -3), ("send", 0, 0), ("ry", 1, "-", 4), ("send", 0, 1), ("send", 0, 2), ("send", 0, 3), ("gx", 1, "+", 3),
    ("gx2", 1, "-", -2), ("qy", 1, 2, "-", 4), ("send", 0, 4), ("gx2", 1, "+", 2), ("gx", 1, "-", 3), ("send", 0, 5),
    ("gx2", 1, "+", -3), ("send", 0, 6), ("send", 0, 7), ("proj", 1), ("gx", 1, "-", 4), ("send", 1, 0), ("gx", 1, "+", 4),
    ("gx2", 1, "-", 3), ("send", 1, 1), ("send", 1, 2), ("send", 1, 3), ("gx2", 1, "-", 4), ("send", 1, 4), ("send", 1, 5),
    ("send", 1, 6), ("send", 1, 7), ("proj", 2), ("send", 2, 0), ("send", 2, 1), ("send", 2, 2), ("send", 2, 3),
    ("send", 2, 4), ("send", 2, 5), ("send", 2, 6), ("send", 2, 7), ("pw", 1),
)
ONWARD = {"+": (0, -1, 2, -3), "-": (1, -2, 3, 4)}


def sign(s):
    return 1 if s == "+" else -1


def kernel(
    img_hbm, imod_ref, cap_hbm, cmod_hbm, owner_ref, wimg_hbm, wtxt_hbm, igain_ref, tgain_ref,
    oimg_ref, ocap_ref,
    img_v, cap_v, cmod_v, mod3, modrow, img_in, txt_in, wt, wi, place_t, picks, onehot3, counts_out, counts_in,
    out_buf, in_buf, qkv, ret_out, ret_in, bias,
    loc_sem, rsem, ssem, asem,
):
    dp = lax.axis_index("dp")
    x, y, c = dp // (NY * NC), (dp // NC) % NY, dp % NC

    def at(xx, yy, cc):
        return (xx * NY + yy) * NC + cc

    def xs(d):
        return (x + d + NX) % NX

    def ys(d):
        return (y + d + NY) % NY

    dev = {
        "x+": at(xs(1), y, c), "x-": at(xs(-1), y, c),
        "y+": at(x, ys(1), c), "y-": at(x, ys(-1), c),
        "p": at(x, y, 1 - c),
    }
    weights = (wt, wi)

    loads = []
    for i, (src, dst) in enumerate((
        (wtxt_hbm, wt.at[x, y, c]), (wimg_hbm, wi.at[x, y, c]),
        (cmod_hbm, cmod_v), (cap_hbm, cap_v), (img_hbm, img_v),
    )):
        copy = pltpu.make_async_copy(src, dst, loc_sem.at[i])
        copy.start()
        loads.append(copy)

    barrier = pltpu.get_barrier_semaphore()
    for d in dev.values():
        pl.semaphore_signal(barrier, inc=1, device_id={"dp": d}, device_id_type=MESH)

    def ypiece(t, xx, yy):
        return weights[t].at[xx, yy, c, :, 16:48, :]

    def yhalf(t, xx, yy, s):
        lo = 16 if s == "+" else 32
        return weights[t].at[xx, yy, c, :, lo : lo + 16, :]

    def xpiece(t, xx, yy):
        return weights[t].at[xx, yy, c, :, 0:16, :]

    names = {}

    def sem(t, name):
        return rsem.at[t, names.setdefault(name, len(names))]

    def send(t, to, piece, name, source=None):
        kind = ("gx", "rx", "ry", "qy", "p").index("gx" if name[0] == "gx2" else "rx" if name[0] == "rx2" else name[0])
        pltpu.make_async_remote_copy(
            src_ref=piece if source is None else source, dst_ref=piece, send_sem=ssem.at[t, kind], recv_sem=sem(t, name),
            device_id={"dp": dev[to]}, device_id_type=MESH,
        ).start()

    def recv(t, piece, name):
        pltpu.make_async_copy(piece, piece, sem(t, name)).wait()

    def weights_sent(t):
        w = weights[t]
        for kind, piece in enumerate((
            w.at[0:2, :, 0], w.at[0, 0, 0], w.at[0:2, 0:7, 0, :, 0:16, :], w.at[:, 0:7, 0, :, 0:16, :], w.at[:, :, 0],
        )):
            pltpu.make_async_copy(piece, piece, ssem.at[t, kind]).wait()

    y4 = [0, 0]

    def s0(t):
        shard = (wtxt_hbm, wimg_hbm)[t]
        own_y, own_x = ypiece(t, x, y), xpiece(t, x, y)
        from_y, from_x = shard.at[:, 16:48, :], shard.at[:, 0:16, :]
        for s in "+-":
            send(t, "x" + s, own_x, ("rx", s), from_x)
            send(t, "y" + s, own_y, ("ry", s, 1), from_y)
            send(t, "x" + s, own_y, ("gx", s, 0), from_y)
        for s in "+-":
            send(t, "y" + s, own_x, ("qy", 0, s, 1), from_x)
        send(t, "p", weights[t].at[x, y, c], ("p",), shard)

    def rx(t, s):
        piece = xpiece(t, xs(-sign(s)), y)
        recv(t, piece, ("rx", s))
        send(t, "p", piece, ("p",))
        if s == "+-"[t]:
            send(t, "x" + s, piece, ("rx2",))
        for s2 in "+-":
            send(t, "y" + s2, piece, ("qy", -sign(s), s2, 1))

    def rx2(t):
        piece = xpiece(t, xs(2), y)
        recv(t, piece, ("rx2",))
        send(t, "p", piece, ("p",))
        for s2 in "+-":
            send(t, "y" + s2, piece, ("qy", 2, s2, 1))

    def qy(t, j, s, d):
        piece = xpiece(t, xs(j), ys(-sign(s) * d))
        recv(t, piece, ("qy", j, s, d))
        send(t, "p", piece, ("p",))
        if d < 3 or (d == 3 and (j in (0, -1)) == (s == "+")):
            send(t, "y" + s, piece, ("qy", j, s, d + 1))

    def ry(t, s, d):
        if d == 4:
            piece = yhalf(t, x, ys(4), s)
            recv(t, piece, ("ry", s, 4))
            send(t, "p", piece, ("p",))
            y4[t] += 1
            if y4[t] == 2:
                for s2 in "+-":
                    send(t, "x" + s2, ypiece(t, x, ys(4)), ("gx", s2, 4))
            return
        dy = -sign(s) * d
        piece = ypiece(t, x, ys(dy))
        recv(t, piece, ("ry", s, d))
        send(t, "p", piece, ("p",))
        if d < 3:
            send(t, "y" + s, piece, ("ry", s, d + 1))
        else:
            send(t, "y" + s, yhalf(t, x, ys(dy), s), ("ry", s, 4))
        for s2 in "+-":
            send(t, "x" + s2, piece, ("gx", s2, dy))

    def gx(t, s, dy):
        piece = ypiece(t, xs(-sign(s)), ys(dy))
        recv(t, piece, ("gx", s, dy))
        send(t, "p", piece, ("p",))
        if dy in ONWARD[s]:
            send(t, "x" + s, piece, ("gx2", s, dy))

    def gx2(t, s, dy):
        piece = ypiece(t, xs(2), ys(dy))
        recv(t, piece, ("gx2", s, dy))
        send(t, "p", piece, ("p",))

    def pw(t):
        recv(t, weights[t].at[:, :, 1 - c], ("p",))
        loads[t].wait()

    bins, width = cap_v.shape
    rows = img_v.shape[0]
    _, _, slot, cols_dev = out_buf.shape
    n_slots = N_DP * slot
    iota = lambda shape, axis: lax.broadcasted_iota(jnp.int32, shape, axis)
    as_bf16 = lambda mask: mask.astype(F32).astype(BF16)

    def route():
        owner = owner_ref[...]
        own_t = as_bf16(owner == iota((N_DP, bins), 0))
        earlier = as_bf16(iota((bins, bins), 0) < iota((bins, bins), 1))
        before = jnp.dot(own_t, earlier, preferred_element_type=F32)
        position = jnp.sum(before * own_t.astype(F32), axis=0, keepdims=True)
        target = owner.astype(F32) * slot + position
        place_t[...] = as_bf16(iota((n_slots, bins), 0).astype(F32) == target)
        target_col = jnp.broadcast_to(target, (128, bins)).T[:, 0:1]
        picks[...] = as_bf16(iota((bins, n_slots), 1).astype(F32) == target_col)
        owner_col = jnp.broadcast_to(owner.astype(F32), (128, bins)).T[:, 0:1]
        onehot3[...] = as_bf16((iota((bins, 3 * N_DP), 1) % N_DP).astype(F32) == owner_col)
        counts = jnp.dot(own_t, jnp.ones((bins, 128), BF16), preferred_element_type=F32)
        counts_out[...] = counts.reshape(N_DP, 1, 128)

    tiles = width // 128

    def split(lo, n):
        @pl.loop(lo, lo + n)
        def _(k):
            lanes = pl.ds(pl.multiple_of(k * 128, 128), 128)
            for j in (0, 1):
                value = cmod_v[pl.ds(2 * k + j, N_DP, stride=2 * tiles), :]
                high = value.astype(BF16)
                rest = value - high.astype(F32)
                mid = rest.astype(BF16)
                low = (rest - mid.astype(F32)).astype(BF16)
                mod3[j, 0:N_DP, lanes] = high
                mod3[j, N_DP : 2 * N_DP, lanes] = mid
                mod3[j, 2 * N_DP :, lanes] = low

    def mods(lo, n):
        @pl.loop(lo, lo + n)
        def _(i):
            lanes = pl.ds(pl.multiple_of(i * 256, 256), 256)
            for j in (0, 1):
                modrow[j, :, lanes] = jnp.dot(onehot3[...], mod3[j, :, lanes], preferred_element_type=F32)

    def norm(values):
        values = values - jnp.mean(values, axis=-1, keepdims=True)
        var = jnp.mean(values * values, axis=-1, keepdims=True)
        return values * lax.rsqrt(var + 1e-06)

    def lnt(lo, n):
        @pl.loop(lo, lo + n)
        def _(i):
            r = pl.ds(pl.multiple_of(i * 16, 16), 16)
            values = norm(cap_v[r, :].astype(F32))
            txt_in[r, :] = (values * (1.0 + modrow[1, r, :]) + modrow[0, r, :]).astype(BF16)

    def lni(lo, n):
        @pl.loop(lo, lo + n)
        def _(i):
            r = pl.ds(pl.multiple_of(i * 16, 16), 16)
            values = norm(img_v[r, :].astype(F32))
            img_in[r, :] = (values * (1.0 + imod_ref[0, 1:2, :]) + imod_ref[0, 0:1, :]).astype(BF16)

    def project(left, t, p, gain_ref):
        total = None
        for xx in range(NX):
            w = weights[t][xx, :, :, p, :, :].reshape(width // NX, cols_dev)
            part = jnp.dot(left[:, xx * (width // NX) : (xx + 1) * (width // NX)], w, preferred_element_type=F32)
            total = part if total is None else total + part
        if p == 2:
            return total.astype(BF16)
        heads = []
        for h in range(cols_dev // HD):
            v = total[:, h * HD : (h + 1) * HD]
            v = v * lax.rsqrt(jnp.mean(v * v, axis=-1, keepdims=True) + 1e-06) * gain_ref[p : p + 1, :]
            heads.append(v)
        return jnp.concatenate(heads, axis=1).astype(BF16)

    def proj(p):
        routed = jnp.dot(place_t[...], project(txt_in, T, p, tgain_ref), preferred_element_type=F32)
        out_buf[p] = routed.reshape(N_DP, slot, cols_dev).astype(BF16)
        keep(out_buf.at[p], in_buf.at[p], 1 + p)

    kept = {}

    def keep(src, dst, k):
        kept[k] = (pltpu.make_async_copy(src.at[dp], dst.at[dp], loc_sem.at[5 + k]), src, dst)
        kept[k][0].start()

    xnear = [xs(dx) * NY for dx in (2, 1, -1, 0)]
    cnear = [1 - c, c]

    def ring(k, yy, n):
        _, src, dst = kept[k]
        for i in range(n):
            d = (xnear[i // NC] + yy) * NC + cnear[i % NC]
            pltpu.make_async_remote_copy(
                src_ref=src.at[d], dst_ref=dst.at[dp], send_sem=asem.at[0, k], recv_sem=asem.at[1, k],
                device_id={"dp": d}, device_id_type=MESH,
            ).start()

    def scatter(k):
        @pl.loop(0, NY - 1)
        def _(a):
            ring(k, ys((4 - (a + 1) // 2) * (1 - 2 * ((a + 1) % 2))), NX * NC)

        ring(k, y, NX * NC - 1)

    def arrived(k):
        own, _, dst = kept[k]
        own.wait()
        pltpu.make_async_copy(dst.at[0 : N_DP - 1], dst.at[0 : N_DP - 1], asem.at[1, k]).wait()

    def left(k):
        src = kept[k][1]
        pltpu.make_async_copy(src.at[0 : N_DP - 1], src.at[0 : N_DP - 1], asem.at[0, k]).wait()

    def attend(h, b, n):
        r = pl.ds(pl.multiple_of(b * n, n), n)
        lanes = slice(h * HD, (h + 1) * HD)
        s = lax.dot_general(
            qkv[0, r, lanes], qkv[1, :, lanes], (((1,), (1,)), ((), ())), preferred_element_type=F32
        )
        s = s + bias[0:1, :]
        top = jnp.max(s, axis=-1, keepdims=True)
        e = jnp.exp2((s - top) * (math.log2(math.e) / math.sqrt(HD)))
        out = jnp.dot(e.astype(BF16), qkv[2, :, lanes], preferred_element_type=F32)
        return out * (1.0 / jnp.sum(e, axis=-1, keepdims=True))

    pl.semaphore_wait(barrier, len(dev))
    moves = dict(s0=s0, rx=rx, rx2=rx2, qy=qy, ry=ry, gx=gx, gx2=gx2, pw=pw)
    work = dict(split=(split, 2, 2), mods=(mods, 1, None), lnt=(lnt, 1, 3), lni=(lni, 1, 4))
    done = dict.fromkeys(work, 0)
    for kind, *args in ORDER:
        if kind == "route":
            route()
        elif kind == "proj":
            proj(*args)
        elif kind == "send":
            p, batch = args
            ring(1 + p, ys((4, 3, -3, 2, -2, 1, -1, 0)[batch]), NX * NC - (batch == NY - 1))
        elif kind in work:
            step, unit, load = work[kind]
            if load is not None and not done[kind]:
                loads[load].wait()
            step(done[kind] * unit, args[0] * unit)
            done[kind] += args[0]
        else:
            moves[kind](*args)
    keep(counts_out, counts_in, 0)
    scatter(0)
    for p in range(3):
        qkv[p, n_slots:, :] = project(img_in, I, p, igain_ref)
    arrived(0)
    filled = counts_in[...].reshape(N_DP, 128)
    filled = jnp.concatenate([filled] * (n_slots // 128), axis=1)
    mine = iota((N_DP, n_slots), 1) // slot == iota((N_DP, n_slots), 0)
    filled = jnp.sum(jnp.where(mine, filled, 0.0), axis=0, keepdims=True)
    place = (iota((1, n_slots), 1) % slot).astype(F32)
    bias[0:1, 0:n_slots] = jnp.where(place < filled, 0.0, -jnp.inf)
    bias[0:1, n_slots:] = jnp.zeros((1, rows), F32)
    for p in range(3):
        arrived(1 + p)
        qkv[p, 0:n_slots, :] = in_buf[p].astype(F32).reshape(n_slots, cols_dev).astype(BF16)
    n = 256
    part = n // slot
    heads = cols_dev // HD
    for h in range(heads):

        @pl.loop(0, n_slots // n)
        def _(b):
            ret_out[h, pl.ds(b * part, part)] = attend(h, b, n).reshape(part, slot, HD).astype(BF16)

        keep(ret_out.at[h], ret_in.at[h], 4 + h)
        scatter(4 + h)

    for h in range(heads):

        @pl.loop(0, rows // n)
        def _(b):
            lanes = slice(h * HD, (h + 1) * HD)
            oimg_ref[pl.ds(pl.multiple_of(b * n, n), n), lanes] = attend(h, n_slots // n + b, n).astype(BF16)

    weights_sent(T)
    weights_sent(I)
    for k in range(4 + heads):
        left(k)
    for h in range(heads):
        arrived(4 + h)
        returned = ret_in[h].astype(F32).reshape(n_slots, HD).astype(BF16)
        ocap_ref[:, h * HD : (h + 1) * HD] = jnp.dot(picks[...], returned, preferred_element_type=F32).astype(BF16)


def finish(image_ref, caption_ref, oimg_ref, ocap_ref):
    oimg_ref[...] = image_ref[...]
    ocap_ref[...] = caption_ref[...]


def body(image_rows, image_mod, caption_rows, caption_mod, row_owner, w_img, w_txt, img_gain, txt_gain):
    rows, width = image_rows.shape
    bins = caption_rows.shape[0]
    slot = 2 * bins // N_DP
    n_slots = N_DP * slot
    depth, _, cols = w_img.shape
    w_img, w_txt = (jnp.transpose(w, (1, 0, 2)) for w in (w_img, w_txt))
    mods = caption_mod.reshape(N_DP, 2, width // 128, 128).transpose(0, 2, 1, 3).reshape(-1, 128)
    vmem = pl.BlockSpec(memory_space=pltpu.VMEM)
    hbm = pl.BlockSpec(memory_space=pl.ANY)
    outs = pl.pallas_call(
        kernel,
        out_shape=(
            jax.ShapeDtypeStruct((rows, cols), BF16),
            jax.ShapeDtypeStruct((bins, cols), BF16),
        ),
        in_specs=[hbm, vmem, hbm, hbm, vmem, hbm, hbm, vmem, vmem],
        out_specs=(vmem, vmem),
        scratch_shapes=[
            pltpu.VMEM((rows, width), BF16),
            pltpu.VMEM((bins, width), BF16),
            pltpu.VMEM(mods.shape, F32),
            pltpu.VMEM((2, 3 * N_DP, width), BF16),
            pltpu.VMEM((2, bins, width), F32),
            pltpu.VMEM((rows, width), BF16),
            pltpu.VMEM((bins, width), BF16),
            pltpu.VMEM((NX, NY, NC, 3, depth, cols), BF16),
            pltpu.VMEM((NX, NY, NC, 3, depth, cols), BF16),
            pltpu.VMEM((n_slots, bins), BF16),
            pltpu.VMEM((bins, n_slots), BF16),
            pltpu.VMEM((bins, 3 * N_DP), BF16),
            pltpu.VMEM((N_DP, 1, 128), F32),
            pltpu.VMEM((N_DP, 1, 128), F32),
            pltpu.VMEM((3, N_DP, slot, cols), BF16),
            pltpu.VMEM((3, N_DP, slot, cols), BF16),
            pltpu.VMEM((3, n_slots + rows, cols), BF16),
            pltpu.VMEM((cols // HD, N_DP, slot, HD), BF16),
            pltpu.VMEM((cols // HD, N_DP, slot, HD), BF16),
            pltpu.VMEM((8, n_slots + rows), F32),
            pltpu.SemaphoreType.DMA((16,)),
            pltpu.SemaphoreType.DMA((2, 64)),
            pltpu.SemaphoreType.DMA((2, 5)),
            pltpu.SemaphoreType.DMA((2, 6)),
        ],
        compiler_params=pltpu.CompilerParams(
            collective_id=0, has_side_effects=True, vmem_limit_bytes=60 * 1024 * 1024
        ),
        name="block",
    )(image_rows, image_mod, caption_rows, mods, row_owner.T, w_img, w_txt, img_gain, txt_gain)
    return pl.pallas_call(
        finish,
        out_shape=tuple(jax.ShapeDtypeStruct(o.shape, o.dtype) for o in outs),
        in_specs=[vmem, vmem],
        out_specs=(vmem, vmem),
        compiler_params=pltpu.CompilerParams(vmem_limit_bytes=60 * 1024 * 1024),
        name="finish",
    )(*outs)


def solution(mesh):
    in_specs = (
        P("dp", None),
        P("dp", None, None),
        P("dp", None),
        P(),
        P("dp", None),
        P("dp", None, "tensor"),
        P("dp", None, "tensor"),
        P(),
        P(),
    )
    out_specs = (P("dp", "tensor"), P("dp", "tensor"))
    return jax.shard_map(body, mesh=mesh, in_specs=in_specs, out_specs=out_specs, check_vma=False)
```

```python
import math

import jax
import jax.numpy as jnp
from jax import lax
from jax.experimental import pallas as pl
from jax.experimental.pallas import tpu as pltpu
from jax.sharding import PartitionSpec as P

MESH = pl.DeviceIdType.MESH
HD = 128
NX, NY, NC = 4, 8, 2
N_DP = NX * NY * NC
F32 = jnp.float32
BF16 = jnp.bfloat16
T, I = 0, 1

ORDER = (
    ("s0", 0), ("s0", 1), ("route", 1), ("split", 10), ("rx", 0, "+"), ("rx", 0, "-"), ("split", 2), ("mods", 1),
    ("ry", 0, "+", 1), ("ry", 0, "-", 1), ("mods", 3), ("gx", 0, "+", 0), ("gx", 0, "-", 0), ("qy", 0, 0, "+", 1),
    ("qy", 0, 0, "-", 1), ("mods", 3), ("rx", 1, "-"), ("mods", 5), ("lnt", 1), ("gx", 1, "-", 0), ("rx", 1, "+"),
    ("lnt", 2), ("rx2", 0), ("qy", 0, -1, "+", 1), ("qy", 0, -1, "-", 1), ("gx", 1, "+", 0), ("lnt", 2),
    ("qy", 0, 1, "+", 1), ("qy", 0, 1, "-", 1), ("gx", 0, "-", -1), ("lnt", 2), ("gx", 0, "+", -1), ("lnt", 2),
    ("ry", 0, "+", 2), ("ry", 0, "-", 2), ("gx", 0, "-", 1), ("lnt", 2), ("gx", 0, "+", 1), ("qy", 0, 0, "+", 2),
    ("qy", 0, 0, "-", 2), ("lnt", 4), ("gx2", 0, "+", 0), ("qy", 1, 0, "+", 1), ("qy", 1, 0, "-", 1), ("lnt", 1), ("lni", 1),
    ("qy", 0, 2, "+", 1), ("qy", 0, 2, "-", 1), ("lni", 2), ("qy", 0, -1, "+", 2), ("qy", 0, -1, "-", 2), ("gx2", 1, "+", 0),
    ("lni", 1), ("gx", 0, "-", -2), ("qy", 0, 1, "+", 2), ("qy", 0, 1, "-", 2), ("lni", 2), ("gx2", 0, "+", -1),
    ("ry", 1, "+", 1), ("qy", 1, 1, "-", 1), ("lni", 2), ("ry", 0, "+", 3), ("ry", 0, "-", 3), ("gx", 0, "-", 2), ("lni", 2),
    ("gx", 0, "+", -2), ("qy", 0, 0, "+", 3), ("qy", 0, 0, "-", 3), ("qy", 1, -1, "-", 1), ("lni", 2), ("gx2", 0, "-", 1),
    ("qy", 1, 0, "-", 2), ("lni", 2), ("gx", 0, "+", 2), ("qy", 0, 2, "+", 2), ("qy", 0, 2, "-", 2), ("lni", 1),
    ("gx2", 0, "-", -2), ("qy", 0, -1, "+", 3), ("qy", 0, -1, "-", 3), ("lni", 2), ("qy", 0, 1, "+", 3),
    ("qy", 0, 1, "-", 3), ("ry", 1, "-", 1), ("qy", 1, 1, "+", 1), ("lni", 2), ("qy", 1, -1, "+", 1), ("gx", 1, "-", -1),
    ("lni", 2), ("ry", 0, "-", 4), ("gx", 0, "+", -3), ("rx2", 1), ("lni", 2), ("ry", 0, "+", 4), ("gx", 0, "-", -3),
    ("qy", 1, 0, "+", 2), ("qy", 1, 1, "-", 2), ("lni", 2), ("gx", 0, "+", 3), ("qy", 0, 0, "+", 4), ("qy", 1, -1, "-", 2),
    ("lni", 1), ("gx", 0, "-", 3), ("qy", 0, 2, "+", 3), ("qy", 0, 2, "-", 3), ("lni", 2), ("qy", 0, -1, "+", 4),
    ("qy", 0, 1, "-", 4), ("gx2", 0, "+", 2), ("gx", 1, "+", -1), ("qy", 1, 0, "-", 3), ("lni", 2), ("gx", 1, "-", 1),
    ("qy", 1, 1, "+", 2), ("lni", 2), ("ry", 1, "+", 2), ("gx", 1, "+", 1), ("qy", 1, -1, "+", 2), ("gx", 0, "-", 4),
    ("qy", 1, 2, "-", 1), ("qy", 1, 2, "+", 1), ("gx2", 0, "+", -3), ("qy", 1, 1, "-", 3), ("qy", 1, 0, "+", 3),
    ("gx2", 0, "-", 3), ("ry", 1, "-", 2), ("qy", 1, -1, "-", 3), ("gx", 0, "+", 4), ("qy", 0, 2, "-", 4),
    ("qy", 1, 1, "+", 3), ("gx2", 1, "-", 1), ("qy", 1, 2, "-", 2), ("gx2", 1, "+", -1), ("ry", 1, "+", 3),
    ("qy", 1, 1, "-", 4), ("qy", 1, -1, "+", 3), ("gx", 1, "-", -2), ("gx", 1, "+", -2), ("qy", 1, 2, "+", 2),
    ("gx2", 0, "-", 4), ("ry", 1, "-", 3), ("qy", 1, 0, "+", 4), ("gx", 1, "+", 2), ("qy", 1, 2, "-", 3), ("gx", 1, "-", 2),
    ("ry", 1, "+", 4), ("pw", 0), ("proj", 0), ("qy", 1, -1, "+", 4), ("gx", 1, "+", -3), ("qy", 1, 2, "+", 3),
    ("gx", 1, "-", -3), ("send", 0, 0), ("ry", 1, "-", 4), ("send", 0, 1), ("send", 0, 2), ("send", 0, 3), ("gx", 1, "+", 3),
    ("gx2", 1, "-", -2), ("qy", 1, 2, "-", 4), ("send", 0, 4), ("gx2", 1, "+", 2), ("gx", 1, "-", 3), ("send", 0, 5),
    ("gx2", 1, "+", -3), ("send", 0, 6), ("send", 0, 7), ("proj", 1), ("gx", 1, "-", 4), ("send", 1, 0), ("gx", 1, "+", 4),
    ("gx2", 1, "-", 3), ("send", 1, 1), ("send", 1, 2), ("send", 1, 3), ("gx2", 1, "-", 4), ("send", 1, 4), ("send", 1, 5),
    ("send", 1, 6), ("send", 1, 7), ("proj", 2), ("send", 2, 0), ("send", 2, 1), ("send", 2, 2), ("send", 2, 3),
    ("send", 2, 4), ("send", 2, 5), ("send", 2, 6), ("send", 2, 7), ("pw", 1),
)
ONWARD = {"+": (0, -1, 2, -3), "-": (1, -2, 3, 4)}


def sign(s):
    return 1 if s == "+" else -1


def kernel(
    img_hbm, imod_ref, cap_hbm, cmod_hbm, owner_ref, wimg_hbm, wtxt_hbm, igain_ref, tgain_ref,
    oimg_ref, ocap_ref,
    img_v, cap_v, cmod_v, mod3, modrow, img_in, txt_in, wt, wi, place_t, picks, onehot3, counts_out, counts_in,
    out_buf, in_buf, qkv, ret_out, ret_in, bias,
    loc_sem, rsem, ssem, asem,
):
    dp = lax.axis_index("dp")
    x, y, c = dp // (NY * NC), (dp // NC) % NY, dp % NC

    def at(xx, yy, cc):
        return (xx * NY + yy) * NC + cc

    def xs(d):
        return (x + d + NX) % NX

    def ys(d):
        return (y + d + NY) % NY

    dev = {
        "x+": at(xs(1), y, c), "x-": at(xs(-1), y, c),
        "y+": at(x, ys(1), c), "y-": at(x, ys(-1), c),
        "p": at(x, y, 1 - c),
    }
    weights = (wt, wi)

    loads = []
    for i, (src, dst) in enumerate((
        (wtxt_hbm, wt.at[x, y, c]), (wimg_hbm, wi.at[x, y, c]),
        (cmod_hbm, cmod_v), (cap_hbm, cap_v), (img_hbm, img_v),
    )):
        copy = pltpu.make_async_copy(src, dst, loc_sem.at[i])
        copy.start()
        loads.append(copy)

    barrier = pltpu.get_barrier_semaphore()
    for d in dev.values():
        pl.semaphore_signal(barrier, inc=1, device_id={"dp": d}, device_id_type=MESH)

    def ypiece(t, xx, yy):
        return weights[t].at[xx, yy, c, :, 16:48, :]

    def yhalf(t, xx, yy, s):
        lo = 16 if s == "+" else 32
        return weights[t].at[xx, yy, c, :, lo : lo + 16, :]

    def xpiece(t, xx, yy):
        return weights[t].at[xx, yy, c, :, 0:16, :]

    names = {}

    def sem(t, name):
        return rsem.at[t, names.setdefault(name, len(names))]

    def send(t, to, piece, name, source=None):
        kind = ("gx", "rx", "ry", "qy", "p").index("gx" if name[0] == "gx2" else "rx" if name[0] == "rx2" else name[0])
        pltpu.make_async_remote_copy(
            src_ref=piece if source is None else source, dst_ref=piece, send_sem=ssem.at[t, kind], recv_sem=sem(t, name),
            device_id={"dp": dev[to]}, device_id_type=MESH,
        ).start()

    def recv(t, piece, name):
        pltpu.make_async_copy(piece, piece, sem(t, name)).wait()

    def weights_sent(t):
        w = weights[t]
        for kind, piece in enumerate((
            w.at[0:2, :, 0], w.at[0, 0, 0], w.at[0:2, 0:7, 0, :, 0:16, :], w.at[:, 0:7, 0, :, 0:16, :], w.at[:, :, 0],
        )):
            pltpu.make_async_copy(piece, piece, ssem.at[t, kind]).wait()

    y4 = [0, 0]

    def s0(t):
        shard = (wtxt_hbm, wimg_hbm)[t]
        own_y, own_x = ypiece(t, x, y), xpiece(t, x, y)
        from_y, from_x = shard.at[:, 16:48, :], shard.at[:, 0:16, :]
        for s in "+-":
            send(t, "x" + s, own_x, ("rx", s), from_x)
            send(t, "y" + s, own_y, ("ry", s, 1), from_y)
            send(t, "x" + s, own_y, ("gx", s, 0), from_y)
        for s in "+-":
            send(t, "y" + s, own_x, ("qy", 0, s, 1), from_x)
        send(t, "p", weights[t].at[x, y, c], ("p",), shard)

    def rx(t, s):
        piece = xpiece(t, xs(-sign(s)), y)
        recv(t, piece, ("rx", s))
        send(t, "p", piece, ("p",))
        if s == "+-"[t]:
            send(t, "x" + s, piece, ("rx2",))
        for s2 in "+-":
            send(t, "y" + s2, piece, ("qy", -sign(s), s2, 1))

    def rx2(t):
        piece = xpiece(t, xs(2), y)
        recv(t, piece, ("rx2",))
        send(t, "p", piece, ("p",))
        for s2 in "+-":
            send(t, "y" + s2, piece, ("qy", 2, s2, 1))

    def qy(t, j, s, d):
        piece = xpiece(t, xs(j), ys(-sign(s) * d))
        recv(t, piece, ("qy", j, s, d))
        send(t, "p", piece, ("p",))
        if d < 3 or (d == 3 and (j in (0, -1)) == (s == "+")):
            send(t, "y" + s, piece, ("qy", j, s, d + 1))

    def ry(t, s, d):
        if d == 4:
            piece = yhalf(t, x, ys(4), s)
            recv(t, piece, ("ry", s, 4))
            send(t, "p", piece, ("p",))
            y4[t] += 1
            if y4[t] == 2:
                for s2 in "+-":
                    send(t, "x" + s2, ypiece(t, x, ys(4)), ("gx", s2, 4))
            return
        dy = -sign(s) * d
        piece = ypiece(t, x, ys(dy))
        recv(t, piece, ("ry", s, d))
        send(t, "p", piece, ("p",))
        if d < 3:
            send(t, "y" + s, piece, ("ry", s, d + 1))
        else:
            send(t, "y" + s, yhalf(t, x, ys(dy), s), ("ry", s, 4))
        for s2 in "+-":
            send(t, "x" + s2, piece, ("gx", s2, dy))

    def gx(t, s, dy):
        piece = ypiece(t, xs(-sign(s)), ys(dy))
        recv(t, piece, ("gx", s, dy))
        send(t, "p", piece, ("p",))
        if dy in ONWARD[s]:
            send(t, "x" + s, piece, ("gx2", s, dy))

    def gx2(t, s, dy):
        piece = ypiece(t, xs(2), ys(dy))
        recv(t, piece, ("gx2", s, dy))
        send(t, "p", piece, ("p",))

    def pw(t):
        recv(t, weights[t].at[:, :, 1 - c], ("p",))
        loads[t].wait()

    bins, width = cap_v.shape
    rows = img_v.shape[0]
    _, _, slot, cols_dev = out_buf.shape
    n_slots = N_DP * slot
    iota = lambda shape, axis: lax.broadcasted_iota(jnp.int32, shape, axis)
    as_bf16 = lambda mask: mask.astype(F32).astype(BF16)

    def route():
        owner = owner_ref[...]
        own_t = as_bf16(owner == iota((N_DP, bins), 0))
        earlier = as_bf16(iota((bins, bins), 0) < iota((bins, bins), 1))
        before = jnp.dot(own_t, earlier, preferred_element_type=F32)
        position = jnp.sum(before * own_t.astype(F32), axis=0, keepdims=True)
        target = owner.astype(F32) * slot + position
        place_t[...] = as_bf16(iota((n_slots, bins), 0).astype(F32) == target)
        target_col = jnp.broadcast_to(target, (128, bins)).T[:, 0:1]
        picks[...] = as_bf16(iota((bins, n_slots), 1).astype(F32) == target_col)
        owner_col = jnp.broadcast_to(owner.astype(F32), (128, bins)).T[:, 0:1]
        onehot3[...] = as_bf16((iota((bins, 3 * N_DP), 1) % N_DP).astype(F32) == owner_col)
        counts = jnp.dot(own_t, jnp.ones((bins, 128), BF16), preferred_element_type=F32)
        counts_out[...] = counts.reshape(N_DP, 1, 128)

    tiles = width // 128

    def split(lo, n):
        @pl.loop(lo, lo + n)
        def _(k):
            lanes = pl.ds(pl.multiple_of(k * 128, 128), 128)
            for j in (0, 1):
                value = cmod_v[pl.ds(2 * k + j, N_DP, stride=2 * tiles), :]
                high = value.astype(BF16)
                rest = value - high.astype(F32)
                mid = rest.astype(BF16)
                low = (rest - mid.astype(F32)).astype(BF16)
                mod3[j, 0:N_DP, lanes] = high
                mod3[j, N_DP : 2 * N_DP, lanes] = mid
                mod3[j, 2 * N_DP :, lanes] = low

    def mods(lo, n):
        @pl.loop(lo, lo + n)
        def _(i):
            lanes = pl.ds(pl.multiple_of(i * 256, 256), 256)
            for j in (0, 1):
                modrow[j, :, lanes] = jnp.dot(onehot3[...], mod3[j, :, lanes], preferred_element_type=F32)

    def norm(values):
        values = values - jnp.mean(values, axis=-1, keepdims=True)
        var = jnp.mean(values * values, axis=-1, keepdims=True)
        return values * lax.rsqrt(var + 1e-06)

    def lnt(lo, n):
        @pl.loop(lo, lo + n)
        def _(i):
            r = pl.ds(pl.multiple_of(i * 16, 16), 16)
            values = norm(cap_v[r, :].astype(F32))
            txt_in[r, :] = (values * (1.0 + modrow[1, r, :]) + modrow[0, r, :]).astype(BF16)

    def lni(lo, n):
        @pl.loop(lo, lo + n)
        def _(i):
            r = pl.ds(pl.multiple_of(i * 16, 16), 16)
            values = norm(img_v[r, :].astype(F32))
            img_in[r, :] = (values * (1.0 + imod_ref[0, 1:2, :]) + imod_ref[0, 0:1, :]).astype(BF16)

    def project(left, t, p, gain_ref):
        total = None
        for xx in range(NX):
            w = weights[t][xx, :, :, p, :, :].reshape(width // NX, cols_dev)
            part = jnp.dot(left[:, xx * (width // NX) : (xx + 1) * (width // NX)], w, preferred_element_type=F32)
            total = part if total is None else total + part
        if p == 2:
            return total.astype(BF16)
        heads = []
        for h in range(cols_dev // HD):
            v = total[:, h * HD : (h + 1) * HD]
            v = v * lax.rsqrt(jnp.mean(v * v, axis=-1, keepdims=True) + 1e-06) * gain_ref[p : p + 1, :]
            heads.append(v)
        return jnp.concatenate(heads, axis=1).astype(BF16)

    def proj(p):
        routed = jnp.dot(place_t[...], project(txt_in, T, p, tgain_ref), preferred_element_type=F32)
        out_buf[p] = routed.reshape(N_DP, slot, cols_dev).astype(BF16)
        keep(out_buf.at[p], in_buf.at[p], 1 + p)

    kept = {}

    def keep(src, dst, k):
        kept[k] = (pltpu.make_async_copy(src.at[dp], dst.at[dp], loc_sem.at[5 + k]), src, dst)
        kept[k][0].start()

    xnear = [xs(dx) * NY for dx in (2, 1, -1, 0)]
    cnear = [1 - c, c]

    def ring(k, yy, n):
        _, src, dst = kept[k]
        for i in range(n):
            d = (xnear[i // NC] + yy) * NC + cnear[i % NC]
            pltpu.make_async_remote_copy(
                src_ref=src.at[d], dst_ref=dst.at[dp], send_sem=asem.at[0, k], recv_sem=asem.at[1, k],
                device_id={"dp": d}, device_id_type=MESH,
            ).start()

    def scatter(k):
        @pl.loop(0, NY - 1)
        def _(a):
            ring(k, ys((4 - (a + 1) // 2) * (1 - 2 * ((a + 1) % 2))), NX * NC)

        ring(k, y, NX * NC - 1)

    def arrived(k):
        own, _, dst = kept[k]
        own.wait()
        pltpu.make_async_copy(dst.at[0 : N_DP - 1], dst.at[0 : N_DP - 1], asem.at[1, k]).wait()

    def left(k):
        src = kept[k][1]
        pltpu.make_async_copy(src.at[0 : N_DP - 1], src.at[0 : N_DP - 1], asem.at[0, k]).wait()

    def attend(h, b, n):
        r = pl.ds(pl.multiple_of(b * n, n), n)
        lanes = slice(h * HD, (h + 1) * HD)
        s = lax.dot_general(
            qkv[0, r, lanes], qkv[1, :, lanes], (((1,), (1,)), ((), ())), preferred_element_type=F32
        )
        s = s + bias[0:1, :]
        top = jnp.max(s, axis=-1, keepdims=True)
        e = jnp.exp2((s - top) * (math.log2(math.e) / math.sqrt(HD)))
        out = jnp.dot(e.astype(BF16), qkv[2, :, lanes], preferred_element_type=F32)
        return out * (1.0 / jnp.sum(e, axis=-1, keepdims=True))

    pl.semaphore_wait(barrier, len(dev))
    moves = dict(s0=s0, rx=rx, rx2=rx2, qy=qy, ry=ry, gx=gx, gx2=gx2, pw=pw)
    work = dict(split=(split, 2, 2), mods=(mods, 1, None), lnt=(lnt, 1, 3), lni=(lni, 1, 4))
    done = dict.fromkeys(work, 0)
    for kind, *args in ORDER:
        if kind == "route":
            route()
        elif kind == "proj":
            if args == [1]:
                keep(counts_out, counts_in, 0)
                scatter(0)
            proj(*args)
        elif kind == "send":
            p, batch = args
            ring(1 + p, ys((4, 3, -3, 2, -2, 1, -1, 0)[batch]), NX * NC - (batch == NY - 1))
        elif kind in work:
            step, unit, load = work[kind]
            if load is not None and not done[kind]:
                loads[load].wait()
            step(done[kind] * unit, args[0] * unit)
            done[kind] += args[0]
        else:
            moves[kind](*args)
    for p in range(3):
        qkv[p, n_slots:, :] = project(img_in, I, p, igain_ref)
    arrived(0)
    filled = counts_in[...].reshape(N_DP, 128)
    filled = jnp.concatenate([filled] * (n_slots // 128), axis=1)
    mine = iota((N_DP, n_slots), 1) // slot == iota((N_DP, n_slots), 0)
    filled = jnp.sum(jnp.where(mine, filled, 0.0), axis=0, keepdims=True)
    place = (iota((1, n_slots), 1) % slot).astype(F32)
    bias[0:1, 0:n_slots] = jnp.where(place < filled, 0.0, -jnp.inf)
    bias[0:1, n_slots:] = jnp.zeros((1, rows), F32)
    for p in range(3):
        arrived(1 + p)
        qkv[p, 0:n_slots, :] = in_buf[p].astype(F32).reshape(n_slots, cols_dev).astype(BF16)
    n = 256
    part = n // slot
    heads = cols_dev // HD
    for h in range(heads):

        @pl.loop(0, n_slots // n)
        def _(b):
            ret_out[h, pl.ds(b * part, part)] = attend(h, b, n).reshape(part, slot, HD).astype(BF16)

        keep(ret_out.at[h], ret_in.at[h], 4 + h)
        scatter(4 + h)

    for h in range(heads):

        @pl.loop(0, rows // n)
        def _(b):
            lanes = slice(h * HD, (h + 1) * HD)
            oimg_ref[pl.ds(pl.multiple_of(b * n, n), n), lanes] = attend(h, n_slots // n + b, n).astype(BF16)

    for h in range(heads):
        arrived(4 + h)
        returned = ret_in[h].astype(F32).reshape(n_slots, HD).astype(BF16)
        ocap_ref[:, h * HD : (h + 1) * HD] = jnp.dot(picks[...], returned, preferred_element_type=F32).astype(BF16)
    weights_sent(T)
    weights_sent(I)
    for k in range(4 + heads):
        left(k)


def finish(image_ref, caption_ref, oimg_ref, ocap_ref):
    oimg_ref[...] = image_ref[...]
    ocap_ref[...] = caption_ref[...]


def body(image_rows, image_mod, caption_rows, caption_mod, row_owner, w_img, w_txt, img_gain, txt_gain):
    rows, width = image_rows.shape
    bins = caption_rows.shape[0]
    slot = 2 * bins // N_DP
    n_slots = N_DP * slot
    depth, _, cols = w_img.shape
    w_img, w_txt = (jnp.transpose(w, (1, 0, 2)) for w in (w_img, w_txt))
    mods = caption_mod.reshape(N_DP, 2, width // 128, 128).transpose(0, 2, 1, 3).reshape(-1, 128)
    vmem = pl.BlockSpec(memory_space=pltpu.VMEM)
    hbm = pl.BlockSpec(memory_space=pl.ANY)
    outs = pl.pallas_call(
        kernel,
        out_shape=(
            jax.ShapeDtypeStruct((rows, cols), BF16),
            jax.ShapeDtypeStruct((bins, cols), BF16),
        ),
        in_specs=[hbm, vmem, hbm, hbm, vmem, hbm, hbm, vmem, vmem],
        out_specs=(vmem, vmem),
        scratch_shapes=[
            pltpu.VMEM((rows, width), BF16),
            pltpu.VMEM((bins, width), BF16),
            pltpu.VMEM(mods.shape, F32),
            pltpu.VMEM((2, 3 * N_DP, width), BF16),
            pltpu.VMEM((2, bins, width), F32),
            pltpu.VMEM((rows, width), BF16),
            pltpu.VMEM((bins, width), BF16),
            pltpu.VMEM((NX, NY, NC, 3, depth, cols), BF16),
            pltpu.VMEM((NX, NY, NC, 3, depth, cols), BF16),
            pltpu.VMEM((n_slots, bins), BF16),
            pltpu.VMEM((bins, n_slots), BF16),
            pltpu.VMEM((bins, 3 * N_DP), BF16),
            pltpu.VMEM((N_DP, 1, 128), F32),
            pltpu.VMEM((N_DP, 1, 128), F32),
            pltpu.VMEM((3, N_DP, slot, cols), BF16),
            pltpu.VMEM((3, N_DP, slot, cols), BF16),
            pltpu.VMEM((3, n_slots + rows, cols), BF16),
            pltpu.VMEM((cols // HD, N_DP, slot, HD), BF16),
            pltpu.VMEM((cols // HD, N_DP, slot, HD), BF16),
            pltpu.VMEM((8, n_slots + rows), F32),
            pltpu.SemaphoreType.DMA((16,)),
            pltpu.SemaphoreType.DMA((2, 64)),
            pltpu.SemaphoreType.DMA((2, 5)),
            pltpu.SemaphoreType.DMA((2, 6)),
        ],
        compiler_params=pltpu.CompilerParams(
            collective_id=0, has_side_effects=True, vmem_limit_bytes=60 * 1024 * 1024
        ),
        name="block",
    )(image_rows, image_mod, caption_rows, mods, row_owner.T, w_img, w_txt, img_gain, txt_gain)
    return pl.pallas_call(
        finish,
        out_shape=tuple(jax.ShapeDtypeStruct(o.shape, o.dtype) for o in outs),
        in_specs=[vmem, vmem],
        out_specs=(vmem, vmem),
        compiler_params=pltpu.CompilerParams(vmem_limit_bytes=60 * 1024 * 1024),
        name="finish",
    )(*outs)


def solution(mesh):
    in_specs = (
        P("dp", None),
        P("dp", None, None),
        P("dp", None),
        P(),
        P("dp", None),
        P("dp", None, "tensor"),
        P("dp", None, "tensor"),
        P(),
        P(),
    )
    out_specs = (P("dp", "tensor"), P("dp", "tensor"))
    return jax.shard_map(body, mesh=mesh, in_specs=in_specs, out_specs=out_specs, check_vma=False)
```
